32 devices in a mesh: half: 2 (over x), grp: 4 (over z), tile: 4 (over y, core).
Axes of the slice: x: 2, y: 2, z: 4, core: 2. Of those that a mesh axis runs over, the one named last changes fastest.
Arguments:
- core_tensor: bfloat16 [256, 96, 160], P(('half', 'grp', 'tile')), may hold values from -0.109375 to 0.109375
- term_operators: bfloat16 [32, 8, 8, 8], P(('half', 'grp', 'tile')), may hold values from -2 to 2
- block_terms: int32 [32, 8], P(('half', 'grp', 'tile')), may hold values from 0 to 8, as said below
- orbitals: bfloat16 [1024, 256, 256], P(('half', 'grp'), 'tile'), may hold values from -6 to 6
- potential: float32 [2, 8, 1024, 256], P(None, None, ('half', 'grp'), 'tile'), may hold values from -2.5 to 2.5
- kinetic: bfloat16 [1024, 1024], replicated, may hold values from -0.1875 to 0.1875
Outputs:
- h_orbitals: bfloat16 [1024, 256, 256], P(('half', 'grp'), 'tile')
The draws below stay inside these ranges and needn't reach their ends.
Inputs may be any that keep to these rules, and one draw needn't show every extreme that they name: `block_terms`: each row lists distinct terms in its first slots and 8 in all later slots; every row lists at least one term, and some row lists 8 terms.
All inputs are finite; a program needn't handle non-finite values.
Results may differ from the reference program's by a relative error of at most 0.0056.
Values may be sent and summed in bfloat16 or wider, within the bound.
No kernel may reach another device: no remote copies, remote signals or barrier semaphores. Data moves between devices by JAX's collectives and lax.ppermute only.
A program may use at most 128 MiB of HBM per device.

```python
import jax
import jax.numpy as jnp
from jax import lax

NA = 160
NB = 96
X = 1024
Y = 256
TERMS = 8
SLOTS = 8
R_DEV = 8
TILES = 32
R = 256
W = 256


def draw_block_terms(key, part):
    key_count, key_full, key_order = jax.random.split(jax.random.fold_in(key, 17), 3)
    levels = jax.random.randint(key_count, (TILES,), 0, 64)
    counts = 1 + levels * levels * (SLOTS - 1) // 4096
    full_tile = jax.random.randint(key_full, (), 0, TILES)
    counts = jnp.where(jnp.arange(TILES) == full_tile, SLOTS, counts)
    row_keys = jax.random.split(key_order, TILES)

    def row_order(row_key):
        return jax.random.permutation(row_key, TERMS)
    orders = jax.vmap(row_order)(row_keys)[:, :SLOTS]
    slots = jnp.arange(SLOTS)
    return jnp.where(slots[None, :] < counts[:, None], orders, TERMS).astype(jnp.int32)


def shard_levels(key, dims, cuts, least, largest):
    level, own = 1.0, jax.random.fold_in(key, 6)
    for axis_at, parts in cuts:
        steps = jnp.exp(jax.random.uniform(jax.random.fold_in(own, axis_at), (parts,), jnp.float32, least / len(cuts), largest / len(cuts)))
        level = level * jnp.repeat(steps, dims[axis_at] // parts).reshape([-1 if axis == axis_at else 1 for axis in range(len(dims))])
    return level


def centred(key, dims, width, most, cuts=(), kind=jnp.bfloat16):
    array = jax.random.normal(key, dims, jnp.float32) * width
    if len(cuts) > 0:
        array = shard_levels(key, dims, cuts, -0.22, 0.18) * array
    return jnp.clip(array, min=-most, max=most).astype(kind)


def setup_inputs(seed: int = 0) -> dict:
    splits = jax.random.split(jax.random.key(seed), 7)
    core_tensor = centred(splits[0], (R, NB, NA), (4 * NB * R_DEV) ** -0.5, 0.109375, ((0, 32),))
    term_operators = centred(splits[1], (TILES, SLOTS, R_DEV, R_DEV), R_DEV ** -0.5, 2.0, ((0, 32),))
    block_terms = draw_block_terms(jax.random.fold_in(splits[6], 71), 0)
    orbitals = centred(splits[3], (X, Y, W), 1.0, 6.0, ((0, 8), (1, 4)))
    potential = centred(splits[4], (2, TERMS, X, Y), 0.35, 2.5, ((2, 8), (3, 4)), jnp.float32)
    kinetic = centred(splits[5], (X, X), X ** -0.5, 0.1875)
    return {"core_tensor": core_tensor, "term_operators": term_operators, "block_terms": block_terms, "orbitals": orbitals, "potential": potential, "kinetic": kinetic}


def tile_sums(core_tensor, term_operators, block_terms):
    tiles = term_operators.shape[0]
    rows_tile = term_operators.shape[2]
    width_b = core_tensor.shape[1]
    width_a = core_tensor.shape[2]
    labels = jnp.arange(TERMS, dtype=jnp.int32)
    highest = lax.Precision.HIGHEST

    def per_tile(running, tile_index):
        sum_a, sum_b = running
        start_row = (tile_index * rows_tile).astype(jnp.int32)
        tile_core = lax.dynamic_slice_in_dim(core_tensor, start_row, rows_tile, 0).astype(jnp.float32)
        flat_core = tile_core.reshape(rows_tile, width_b * width_a)
        operators = lax.dynamic_index_in_dim(term_operators, tile_index, 0, keepdims=False).astype(jnp.float32)
        listed = lax.dynamic_index_in_dim(block_terms, tile_index, 0, keepdims=False)
        for slot_index in range(SLOTS):
            def tile_grams(operand):
                mixed_core = jnp.dot(operators[slot_index].T, flat_core, precision=highest).astype(jnp.bfloat16)
                mixed_core = lax.optimization_barrier(mixed_core).astype(jnp.float32)
                mixed_core = mixed_core.reshape(rows_tile, width_b, width_a)
                gram_a = jnp.einsum('rba,rbc->ac', tile_core, mixed_core, precision=highest)
                gram_b = jnp.einsum('rba,rda->bd', tile_core, mixed_core, precision=highest)
                return gram_a, gram_b

            def nothing(operand):
                return (jnp.zeros((width_a, width_a), jnp.float32), jnp.zeros((width_b, width_b), jnp.float32))

            gram_a, gram_b = lax.cond(listed[slot_index] < TERMS, tile_grams, nothing, 0)
            chosen = (labels == listed[slot_index]).astype(jnp.float32)
            sum_a = sum_a + chosen[:, None, None] * gram_a
            sum_b = sum_b + chosen[:, None, None] * gram_b
        return (sum_a, sum_b), None

    start_sums = (jnp.zeros((TERMS, width_a, width_a), jnp.float32), jnp.zeros((TERMS, width_b, width_b), jnp.float32))
    (sum_a, sum_b), unused = lax.scan(per_tile, start_sums, jnp.arange(tiles, dtype=jnp.int32))
    return sum_a, sum_b


def point_action(points, weights, stack_a, stack_b):
    width_a = stack_a.shape[0]
    width_b = stack_b.shape[0]
    count_points = points.shape[0]
    prod_a = jnp.dot(points[:, :width_a], stack_a, preferred_element_type=jnp.float32).reshape(count_points, TERMS, width_a)
    prod_b = jnp.dot(points[:, width_a:], stack_b, preferred_element_type=jnp.float32).reshape(count_points, TERMS, width_b)
    act_a = jnp.sum(prod_a * weights[0].T[:, :, None], axis=1)
    act_b = jnp.sum(prod_b * weights[1].T[:, :, None], axis=1)
    return jnp.concatenate([act_a, act_b], axis=1)


def reference(core_tensor, term_operators, block_terms, orbitals, potential, kinetic):
    sum_a, sum_b = tile_sums(core_tensor, term_operators, block_terms)
    mean_a = sum_a.astype(jnp.bfloat16)
    mean_b = sum_b.astype(jnp.bfloat16)
    width_a = mean_a.shape[1]
    width_b = mean_b.shape[1]
    stack_a = jnp.transpose(mean_a, (1, 0, 2)).reshape(width_a, TERMS * width_a)
    stack_b = jnp.transpose(mean_b, (1, 0, 2)).reshape(width_b, TERMS * width_b)
    size_x, size_y, width_all = orbitals.shape
    step_x = 8
    blocks = orbitals.reshape(size_x // step_x, step_x * size_y, width_all)
    weights = potential.reshape(2, TERMS, size_x // step_x, step_x * size_y).transpose(2, 0, 1, 3)

    def per_block(member):
        return point_action(member[0], member[1], stack_a, stack_b)

    action = lax.map(per_block, (blocks, weights)).reshape(size_x, size_y, width_all)
    kinetic_part = jnp.dot(kinetic, orbitals.reshape(size_x, size_y * width_all), preferred_element_type=jnp.float32)
    kinetic_part = kinetic_part.astype(jnp.bfloat16).reshape(size_x, size_y, width_all)
    return (kinetic_part.astype(jnp.float32) + action).astype(jnp.bfloat16)
```

```python
import functools

import jax
import jax.numpy as jnp
from jax import lax
from jax.experimental import pallas as pl
from jax.experimental.pallas import tpu as pltpu
from jax.sharding import PartitionSpec as P


TERMS = 8
GROUP = ("half", "grp")
SIDE = 16
BF = jnp.bfloat16
F32 = jnp.float32


def slot_sums(core_tensor, term_operators, block_terms):
    rows_tile, width_b, width_a = core_tensor.shape
    flat_core = core_tensor.reshape(rows_tile, width_b * width_a)
    listed = block_terms[0]
    live_slots = jnp.sum((listed < TERMS).astype(jnp.int32))
    labels = jnp.arange(TERMS, dtype=jnp.int32)

    def add_slot(slot_index, running):
        sum_a, sum_b = running
        operator = term_operators[0, slot_index]
        mixed_core = jnp.einsum("rs,rq->sq", operator, flat_core, preferred_element_type=F32)
        mixed_core = mixed_core.astype(BF).reshape(rows_tile, width_b, width_a)
        gram_a = jnp.einsum("rba,rbc->ac", core_tensor, mixed_core, preferred_element_type=F32)
        gram_b = jnp.einsum("rba,rda->bd", core_tensor, mixed_core, preferred_element_type=F32)
        chosen = (labels == listed[slot_index]).astype(F32)
        return (sum_a + chosen[:, None, None] * gram_a, sum_b + chosen[:, None, None] * gram_b)

    start_sums = (
        jnp.zeros((TERMS, width_a, width_a), F32),
        jnp.zeros((TERMS, width_b, width_b), F32),
    )
    return lax.fori_loop(0, live_slots, add_slot, start_sums)


def point_action(points, weights, stack_a, stack_b):
    width_a = stack_a.shape[0]
    width_b = stack_b.shape[0]
    count_points = points.shape[0]
    prod_a = jnp.dot(points[:, :width_a], stack_a, preferred_element_type=F32).reshape(
        count_points, TERMS, width_a
    )
    prod_b = jnp.dot(points[:, width_a:], stack_b, preferred_element_type=F32).reshape(
        count_points, TERMS, width_b
    )
    act_a = jnp.sum(prod_a * weights[0].T[:, :, None], axis=1)
    act_b = jnp.sum(prod_b * weights[1].T[:, :, None], axis=1)
    return jnp.concatenate([act_a, act_b], axis=1)


def kinetic_columns(kinetic, orbitals):
    rows_x, rows_y, width_all = orbitals.shape
    groups = lax.axis_size("half") * lax.axis_size("grp")
    columns = rows_y * width_all // groups
    pieces = orbitals.reshape(rows_x, groups, columns)
    applied = jnp.einsum(
        "xz,zik->xik",
        kinetic,
        lax.all_to_all(pieces, GROUP, split_axis=1, concat_axis=0, tiled=True),
        preferred_element_type=F32,
    )
    applied = applied.astype(BF)
    returned = lax.all_to_all(applied, GROUP, split_axis=0, concat_axis=1, tiled=True)
    return returned.reshape(rows_x, rows_y, width_all)


def plain_body(core_tensor, term_operators, block_terms, orbitals, potential, kinetic):
    sum_a, sum_b = slot_sums(core_tensor, term_operators, block_terms)
    total_a, total_b = lax.psum((sum_a, sum_b), ("half", "grp", "tile"))
    mean_a = total_a.astype(BF)
    mean_b = total_b.astype(BF)
    kinetic_part = kinetic_columns(kinetic, orbitals)
    rows_x, rows_y, width_all = orbitals.shape
    width_a = mean_a.shape[1]
    width_b = mean_b.shape[1]
    stack_a = jnp.transpose(mean_a, (1, 0, 2)).reshape(width_a, TERMS * width_a)
    stack_b = jnp.transpose(mean_b, (1, 0, 2)).reshape(width_b, TERMS * width_b)
    points = orbitals.reshape(rows_x * rows_y, width_all)
    weights = potential.reshape(2, TERMS, rows_x * rows_y)
    action = point_action(points, weights, stack_a, stack_b).reshape(rows_x, rows_y, width_all)
    return (kinetic_part.astype(F32) + action).astype(BF)


VMEM = pl.BlockSpec(memory_space=pltpu.VMEM)
SMEM = pl.BlockSpec(memory_space=pltpu.SMEM)


def swap_matrix():
    count = SIDE * SIDE
    row = lax.broadcasted_iota(jnp.int32, (count, count), 0)
    col = lax.broadcasted_iota(jnp.int32, (count, count), 1)
    hit = (row // SIDE == col % SIDE) & (row % SIDE == col // SIDE)
    return jnp.where(hit, 1.0, 0.0).astype(BF)


def slot_kernel(terms_ref, oper_ref, core_ref, out_ref, core_f, core_t, core_p, mixed):
    rows, width_b, width_a = core_ref.shape
    width = out_ref.shape[2]
    slots = terms_ref.shape[1]
    out_ref[...] = jnp.zeros_like(out_ref)
    mixed[...] = jnp.zeros_like(mixed)
    core_p[...] = jnp.zeros_like(core_p)
    core_p[:, :, :width_a] = core_ref[...]
    core_f[...] = core_p[...].astype(F32)
    core_t[...] = jnp.transpose(core_f[...].reshape(rows * width_b, width)).astype(BF)
    live = jnp.int32(0)
    for slot in range(slots):
        live = live + (terms_ref[0, slot] < TERMS).astype(jnp.int32)

    def one_slot(slot, carry):
        def one_block(block, inner):
            start = pl.multiple_of(block * 16, 16)
            source = [core_f[r, pl.ds(start, 16), :] for r in range(rows)]
            for q in range(rows):
                total = source[0] * oper_ref[slot, q]
                for r in range(1, rows):
                    total = total + source[r] * oper_ref[slot, r * rows + q]
                mixed[q, pl.ds(width_a + start, 16), :] = total.astype(BF)
            return inner

        lax.fori_loop(0, width_b // 16, one_block, 0)
        flat = mixed[:, width_a:, :].reshape(rows * width_b, width)
        gram_a = jnp.dot(core_t[:width_a, :], flat, preferred_element_type=F32)
        gram_b = jnp.zeros((width_b, width), F32)
        for q in range(rows):
            gram_b = gram_b + lax.dot_general(
                core_p[q], mixed[q], (((1,), (1,)), ((), ())), preferred_element_type=F32
            )
        term = terms_ref[0, slot]
        out_ref[term, :width_b, :] = (gram_a[:width_b] + gram_b).astype(BF)
        out_ref[term, width_b:, :] = gram_a[width_b:].astype(BF)
        return carry

    lax.fori_loop(0, live, one_slot, 0)


def tile_mean_fields(core_tensor, term_operators, block_terms):
    rows, width_b, width_a = core_tensor.shape
    slots = block_terms.shape[1]
    width = width_a + width_b
    operators = term_operators.astype(F32).reshape(slots, rows * rows)
    return pl.pallas_call(
        slot_kernel,
        out_shape=jax.ShapeDtypeStruct((TERMS, width_a, width), BF),
        in_specs=[SMEM, SMEM, VMEM],
        out_specs=VMEM,
        scratch_shapes=[
            pltpu.VMEM((rows, width_b, width), F32),
            pltpu.VMEM((width, rows * width_b), BF),
            pltpu.VMEM((rows, width_b, width), BF),
            pltpu.VMEM((rows, width, width), BF),
        ],
        cost_estimate=pl.CostEstimate(flops=10**9, bytes_accessed=2 * 10**6, transcendentals=0),
        name="slot_sums",
    )(block_terms, operators, core_tensor)


def exchange(array, axes, flip):
    count = lax.axis_size(axes)
    return lax.ppermute(array, axes, [(i, i ^ flip) for i in range(count)])


def scatter_sum(array, axes, place, flips):
    rows = array.shape[0] // (len(flips) + 1)

    def block(index):
        return lax.dynamic_slice_in_dim(array, index * rows, rows, 0)

    arrived = [exchange(block(place ^ own), axes, flip) for flip, own in flips]
    total = block(place).astype(F32)
    for part in arrived:
        total = total + part.astype(F32)
    return total.astype(BF)


def gather_blocks(array, axes, place, flips):
    rows = array.shape[0]
    whole = jnp.zeros((rows * (len(flips) + 1),) + array.shape[1:], array.dtype)
    arrived = [(own, exchange(array, axes, flip)) for flip, own in flips]
    whole = lax.dynamic_update_slice_in_dim(whole, array, place * rows, 0)
    for own, part in arrived:
        whole = lax.dynamic_update_slice_in_dim(whole, part, (place ^ own) * rows, 0)
    return whole


def bit_flips(bits):
    flips = []
    for own in range(1, 1 << len(bits)):
        flip = sum(1 << bit for at, bit in enumerate(bits) if own >> at & 1)
        flips.append((flip, own))
    return flips


def place_of(index, bits):
    place = jnp.int32(0)
    for at, bit in enumerate(bits):
        place = place | (((index >> bit) & 1) << at)
    return place


def total_mean_fields(partial):
    terms, width_a, width = partial.shape
    group_index = lax.axis_index(GROUP)
    tile_index = lax.axis_index("tile")
    tile_bits = list(range(lax.axis_size("tile").bit_length() - 1))
    group_bits = list(range(lax.axis_size(GROUP).bit_length() - 1))
    far = lax.axis_size("grp").bit_length() - 2
    stages = [("tile", tile_index, tile_bits)]
    stages.append((GROUP, group_index, [bit for bit in group_bits if bit != far]))
    stages.append((GROUP, group_index, [far]))
    array = partial.reshape(terms * width_a, width)
    for axes, index, bits in stages:
        array = scatter_sum(array, axes, place_of(index, bits), bit_flips(bits))
    for axes, index, bits in reversed(stages):
        array = gather_blocks(array, axes, place_of(index, bits), bit_flips(bits))
    return array.reshape(terms, width_a, width)


def action_kernel(points_ref, weight_ref, mean_ref, out_ref, blocks):
    width_a = mean_ref.shape[1]
    rows, width = points_ref.shape
    width_b = width - width_a

    @pl.when(pl.program_id(0) == 0)
    def _():
        lane = lax.broadcasted_iota(jnp.int32, (width_a, width), 1)
        for term in range(TERMS):
            packed = mean_ref[term].astype(F32)
            blocks[term, :width_a, :] = jnp.where(lane < width_a, packed, 0.0).astype(BF)
            blocks[term, width_a:, :] = jnp.where(
                lane[:width_b] < width_a, 0.0, packed[:width_b]
            ).astype(BF)

    step = 256
    for start in range(0, rows, step):
        points = points_ref[start : start + step, :]
        lane = lax.broadcasted_iota(jnp.int32, (step, width), 1)
        total = jnp.zeros((step, width), F32)
        for term in range(TERMS):
            prod = jnp.dot(points, blocks[term], preferred_element_type=F32)
            on_a = weight_ref[start : start + step, term : term + 1]
            on_b = weight_ref[start : start + step, TERMS + term : TERMS + term + 1]
            weight = jnp.where(lane < width_a, on_a, on_b)
            total = total + prod * weight
        out_ref[start : start + step, :] = total


def action_of(orbitals, potential, mean):
    rows_x, rows_y, width = orbitals.shape
    count = rows_x * rows_y
    points = orbitals.reshape(count, width)
    weights = potential.reshape(2 * TERMS, count).T
    step = 512
    action = pl.pallas_call(
        action_kernel,
        grid=(count // step,),
        out_shape=jax.ShapeDtypeStruct((count, width), F32),
        in_specs=[
            pl.BlockSpec((step, width), lambda i: (i, 0)),
            pl.BlockSpec((step, 2 * TERMS), lambda i: (i, 0)),
            pl.BlockSpec(mean.shape, lambda i: (0, 0, 0)),
        ],
        out_specs=pl.BlockSpec((step, width), lambda i: (i, 0)),
        scratch_shapes=[pltpu.VMEM((TERMS, width, width), BF)],
        cost_estimate=pl.CostEstimate(
            flops=2 * count * width * width * TERMS, bytes_accessed=2 * 10**7, transcendentals=0
        ),
        name="action",
    )(points, weights, mean)
    return action.reshape(rows_x, rows_y, width)


def split_kernel(groups, me_ref, orb_ref, *refs):
    outs, rows = refs[:groups], refs[groups]
    rows_x, chunk, width = orb_ref.shape
    per = chunk // groups
    swap = swap_matrix()
    for start in range(0, rows_x, SIDE):
        block = orb_ref[start : start + SIDE].reshape(SIDE * SIDE, width)
        turned = jnp.dot(swap, block, preferred_element_type=F32).astype(BF)
        rows[:, start : start + SIDE, :] = turned.reshape(SIDE, SIDE, width)
    me = me_ref[0]
    for flip in range(groups):
        outs[flip][...] = rows[pl.ds((me ^ flip) * per, per)]


def split_chunk(me, orbitals, chunk_index, chunk, groups):
    rows_x, _, width = orbitals.shape
    piece = (chunk // groups, rows_x, width)
    return pl.pallas_call(
        functools.partial(split_kernel, groups),
        grid=(1,),
        out_shape=[jax.ShapeDtypeStruct(piece, BF)] * groups,
        in_specs=[SMEM, pl.BlockSpec((rows_x, chunk, width), lambda i: (0, chunk_index, 0))],
        out_specs=[pl.BlockSpec(piece, lambda i: (0, 0, 0))] * groups,
        scratch_shapes=[pltpu.VMEM((chunk, rows_x, width), BF)],
        cost_estimate=pl.CostEstimate(
            flops=2 * rows_x * chunk * width * SIDE * SIDE,
            bytes_accessed=4 * rows_x * chunk * width,
            transcendentals=0,
        ),
        name="split",
    )(me, orbitals)


def apply_kernel(groups, me_ref, kin_ref, *refs):
    pieces, outs = refs[:groups], refs[groups : 2 * groups]
    gathered, result = refs[2 * groups :]
    per, rows_x, _ = pieces[0].shape
    size_x = kin_ref.shape[0]
    me = me_ref[0]
    step = 256
    for row in range(per):
        for flip in range(groups):
            start = pl.multiple_of((me ^ flip) * rows_x, rows_x)
            gathered[row, pl.ds(start, rows_x), :] = pieces[flip][row]
        for start in range(0, size_x, step):
            applied = jnp.dot(
                kin_ref[start : start + step, :], gathered[row], preferred_element_type=F32
            )
            result[row, start : start + step, :] = applied.astype(BF)
        for flip in range(groups):
            start = pl.multiple_of((me ^ flip) * rows_x, rows_x)
            outs[flip][row] = result[row, pl.ds(start, rows_x), :]


def apply_chunk(me, kinetic, pieces):
    groups = len(pieces)
    per, rows_x, width = pieces[0].shape
    size_x = kinetic.shape[0]
    return pl.pallas_call(
        functools.partial(apply_kernel, groups),
        out_shape=[jax.ShapeDtypeStruct((per, rows_x, width), BF)] * groups,
        in_specs=[SMEM, VMEM] + [VMEM] * groups,
        out_specs=[VMEM] * groups,
        scratch_shapes=[pltpu.VMEM((per, size_x, width), BF)] * 2,
        cost_estimate=pl.CostEstimate(
            flops=2 * size_x * size_x * per * width, bytes_accessed=4 * 10**6, transcendentals=0
        ),
        name="apply",
    )(me, kinetic, *pieces)


def join_kernel(groups, me_ref, action_ref, *refs):
    pieces = refs[:groups]
    out_ref, rows = refs[-2:]
    per = pieces[0].shape[0]
    step_x, _, width = out_ref.shape
    me = me_ref[0]
    for flip in range(groups):
        rows[pl.ds((me ^ flip) * per, per)] = pieces[flip][...]
    swap = swap_matrix()
    for start in range(0, step_x, SIDE):
        block = rows[:, start : start + SIDE, :].reshape(SIDE * SIDE, width)
        turned = jnp.dot(swap, block, preferred_element_type=F32).reshape(SIDE, SIDE, width)
        out_ref[start : start + SIDE] = (turned + action_ref[start : start + SIDE]).astype(BF)


def join_chunk(me, action, pieces, chunk_index, before):
    groups = len(pieces)
    per, rows_x, width = pieces[0].shape
    chunk = per * groups
    rows_y = action.shape[1]
    step_x = 32
    first = before is None
    block = pl.BlockSpec((step_x, chunk, width), lambda i: (i, chunk_index, 0))
    in_specs = [SMEM, block] + [pl.BlockSpec((per, step_x, width), lambda i: (0, i, 0))] * groups
    operands = [me, action, *pieces]
    aliases = {}
    if not first:
        in_specs.append(pl.BlockSpec(memory_space=pl.ANY))
        aliases = {len(operands): 0}
        operands.append(before)
    return pl.pallas_call(
        functools.partial(join_kernel, groups),
        grid=(rows_x // step_x,),
        out_shape=jax.ShapeDtypeStruct((rows_x, rows_y, width), BF),
        in_specs=in_specs,
        out_specs=block,
        scratch_shapes=[pltpu.VMEM((chunk, step_x, width), BF)],
        input_output_aliases=aliases,
        cost_estimate=pl.CostEstimate(
            flops=2 * rows_x * chunk * width * SIDE * SIDE,
            bytes_accessed=8 * rows_x * chunk * width,
            transcendentals=0,
        ),
        name="join",
    )(*operands)


def exchange_all(pieces):
    groups = len(pieces)
    far = lax.axis_size("grp") // 2
    order = sorted(range(1, groups), key=lambda flip: (flip & far == 0, flip))
    arrived = list(pieces)
    for flip in order:
        arrived[flip] = exchange(pieces[flip], GROUP, flip)
    return arrived


def chunked_body(core_tensor, term_operators, block_terms, orbitals, potential, kinetic):
    _, rows_y, _ = orbitals.shape
    groups = lax.axis_size(GROUP)
    chunk = SIDE
    chunks = rows_y // chunk
    me = lax.axis_index(GROUP).astype(jnp.int32).reshape(1)
    returned = []
    for index in range(chunks):
        pieces = split_chunk(me, orbitals, index, chunk, groups)
        pieces = exchange_all(pieces)
        pieces = apply_chunk(me, kinetic, pieces)
        returned.append(exchange_all(pieces))
    partial = tile_mean_fields(core_tensor, term_operators, block_terms)
    mean = total_mean_fields(partial)
    action = action_of(orbitals, potential, mean)
    result = None
    for index in range(chunks):
        result = join_chunk(me, action, returned[index], index, result)
    return result


def fits(core_tensor, orbitals, mesh):
    rows_x, rows_y, width = orbitals
    groups = mesh.shape["half"] * mesh.shape["grp"]
    tiles = mesh.shape["tile"]
    _, width_b, width_a = core_tensor
    return (
        mesh.shape["half"] == 2
        and mesh.shape["grp"] >= 2
        and groups & (groups - 1) == 0
        and tiles & (tiles - 1) == 0
        and tiles > 1
        and SIDE % groups == 0
        and rows_y % SIDE == 0
        and rows_x % 128 == 0
        and width == width_a + width_b
        and width % 256 == 0
        and width_b % 16 == 0
        and width_a % 16 == 0
        and width_b <= width_a
        and TERMS * width_a % (groups * tiles * 8) == 0
    )


def solution(mesh):
    specs = (
        P(("half", "grp", "tile"), None, None),
        P(("half", "grp", "tile"), None, None, None),
        P(("half", "grp", "tile"), None),
        P(("half", "grp"), "tile", None),
        P(None, None, ("half", "grp"), "tile"),
        P(),
    )

    def build(body):
        return jax.shard_map(body, mesh=mesh, in_specs=specs, out_specs=specs[3], check_vma=False)

    def whole(core_tensor, term_operators, block_terms, orbitals, potential, kinetic):
        args = (core_tensor, term_operators, block_terms, orbitals, potential, kinetic)
        size_x, size_y, width = orbitals.shape
        rows_x = size_x // (mesh.shape["half"] * mesh.shape["grp"])
        rows_y = size_y // mesh.shape["tile"]
        if not fits(core_tensor.shape, (rows_x, rows_y, width), mesh):
            return build(plain_body)(*args)
        return build(chunked_body)(*args)

    return whole
```

```python
import functools

import jax
import jax.numpy as jnp
from jax import lax
from jax.experimental import pallas as pl
from jax.experimental.pallas import tpu as pltpu
from jax.sharding import PartitionSpec as P


TERMS = 8
GROUP = ("half", "grp")
SIDE = 16
BF = jnp.bfloat16
F32 = jnp.float32


def slot_sums(core_tensor, term_operators, block_terms):
    rows_tile, width_b, width_a = core_tensor.shape
    flat_core = core_tensor.reshape(rows_tile, width_b * width_a)
    listed = block_terms[0]
    live_slots = jnp.sum((listed < TERMS).astype(jnp.int32))
    labels = jnp.arange(TERMS, dtype=jnp.int32)

    def add_slot(slot_index, running):
        sum_a, sum_b = running
        operator = term_operators[0, slot_index]
        mixed_core = jnp.einsum("rs,rq->sq", operator, flat_core, preferred_element_type=F32)
        mixed_core = mixed_core.astype(BF).reshape(rows_tile, width_b, width_a)
        gram_a = jnp.einsum("rba,rbc->ac", core_tensor, mixed_core, preferred_element_type=F32)
        gram_b = jnp.einsum("rba,rda->bd", core_tensor, mixed_core, preferred_element_type=F32)
        chosen = (labels == listed[slot_index]).astype(F32)
        return (sum_a + chosen[:, None, None] * gram_a, sum_b + chosen[:, None, None] * gram_b)

    start_sums = (
        jnp.zeros((TERMS, width_a, width_a), F32),
        jnp.zeros((TERMS, width_b, width_b), F32),
    )
    return lax.fori_loop(0, live_slots, add_slot, start_sums)


def point_action(points, weights, stack_a, stack_b):
    width_a = stack_a.shape[0]
    width_b = stack_b.shape[0]
    count_points = points.shape[0]
    prod_a = jnp.dot(points[:, :width_a], stack_a, preferred_element_type=F32).reshape(
        count_points, TERMS, width_a
    )
    prod_b = jnp.dot(points[:, width_a:], stack_b, preferred_element_type=F32).reshape(
        count_points, TERMS, width_b
    )
    act_a = jnp.sum(prod_a * weights[0].T[:, :, None], axis=1)
    act_b = jnp.sum(prod_b * weights[1].T[:, :, None], axis=1)
    return jnp.concatenate([act_a, act_b], axis=1)


def kinetic_columns(kinetic, orbitals):
    rows_x, rows_y, width_all = orbitals.shape
    groups = lax.axis_size("half") * lax.axis_size("grp")
    columns = rows_y * width_all // groups
    pieces = orbitals.reshape(rows_x, groups, columns)
    applied = jnp.einsum(
        "xz,zik->xik",
        kinetic,
        lax.all_to_all(pieces, GROUP, split_axis=1, concat_axis=0, tiled=True),
        preferred_element_type=F32,
    )
    applied = applied.astype(BF)
    returned = lax.all_to_all(applied, GROUP, split_axis=0, concat_axis=1, tiled=True)
    return returned.reshape(rows_x, rows_y, width_all)


def plain_body(core_tensor, term_operators, block_terms, orbitals, potential, kinetic):
    sum_a, sum_b = slot_sums(core_tensor, term_operators, block_terms)
    total_a, total_b = lax.psum((sum_a, sum_b), ("half", "grp", "tile"))
    mean_a = total_a.astype(BF)
    mean_b = total_b.astype(BF)
    kinetic_part = kinetic_columns(kinetic, orbitals)
    rows_x, rows_y, width_all = orbitals.shape
    width_a = mean_a.shape[1]
    width_b = mean_b.shape[1]
    stack_a = jnp.transpose(mean_a, (1, 0, 2)).reshape(width_a, TERMS * width_a)
    stack_b = jnp.transpose(mean_b, (1, 0, 2)).reshape(width_b, TERMS * width_b)
    points = orbitals.reshape(rows_x * rows_y, width_all)
    weights = potential.reshape(2, TERMS, rows_x * rows_y)
    action = point_action(points, weights, stack_a, stack_b).reshape(rows_x, rows_y, width_all)
    return (kinetic_part.astype(F32) + action).astype(BF)


VMEM = pl.BlockSpec(memory_space=pltpu.VMEM)
SMEM = pl.BlockSpec(memory_space=pltpu.SMEM)


def swap_matrix():
    count = SIDE * SIDE
    row = lax.broadcasted_iota(jnp.int32, (count, count), 0)
    col = lax.broadcasted_iota(jnp.int32, (count, count), 1)
    hit = (row // SIDE == col % SIDE) & (row % SIDE == col // SIDE)
    return jnp.where(hit, 1.0, 0.0).astype(BF)


def slot_kernel(terms_ref, oper_ref, core_ref, out_ref, core_f, core_t, core_p, mixed):
    rows, width_b, width_a = core_ref.shape
    width = out_ref.shape[2]
    slots = terms_ref.shape[1]
    out_ref[...] = jnp.zeros_like(out_ref)
    mixed[...] = jnp.zeros_like(mixed)
    core_p[...] = jnp.zeros_like(core_p)
    core_p[:, :, :width_a] = core_ref[...]
    core_f[...] = core_p[...].astype(F32)
    core_t[...] = jnp.transpose(core_f[...].reshape(rows * width_b, width)).astype(BF)
    live = jnp.int32(0)
    for slot in range(slots):
        live = live + (terms_ref[0, slot] < TERMS).astype(jnp.int32)

    def one_slot(slot, carry):
        def one_block(block, inner):
            start = pl.multiple_of(block * 16, 16)
            source = [core_f[r, pl.ds(start, 16), :] for r in range(rows)]
            for q in range(rows):
                total = source[0] * oper_ref[slot, q]
                for r in range(1, rows):
                    total = total + source[r] * oper_ref[slot, r * rows + q]
                mixed[q, pl.ds(width_a + start, 16), :] = total.astype(BF)
            return inner

        lax.fori_loop(0, width_b // 16, one_block, 0)
        flat = mixed[:, width_a:, :].reshape(rows * width_b, width)
        gram_a = jnp.dot(core_t[:width_a, :], flat, preferred_element_type=F32)
        gram_b = jnp.zeros((width_b, width), F32)
        for q in range(rows):
            gram_b = gram_b + lax.dot_general(
                core_p[q], mixed[q], (((1,), (1,)), ((), ())), preferred_element_type=F32
            )
        term = terms_ref[0, slot]
        out_ref[term, :width_b, :] = (gram_a[:width_b] + gram_b).astype(BF)
        out_ref[term, width_b:, :] = gram_a[width_b:].astype(BF)
        return carry

    lax.fori_loop(0, live, one_slot, 0)


def tile_mean_fields(core_tensor, term_operators, block_terms):
    rows, width_b, width_a = core_tensor.shape
    slots = block_terms.shape[1]
    width = width_a + width_b
    operators = term_operators.astype(F32).reshape(slots, rows * rows)
    return pl.pallas_call(
        slot_kernel,
        out_shape=jax.ShapeDtypeStruct((TERMS, width_a, width), BF),
        in_specs=[SMEM, SMEM, VMEM],
        out_specs=VMEM,
        scratch_shapes=[
            pltpu.VMEM((rows, width_b, width), F32),
            pltpu.VMEM((width, rows * width_b), BF),
            pltpu.VMEM((rows, width_b, width), BF),
            pltpu.VMEM((rows, width, width), BF),
        ],
        cost_estimate=pl.CostEstimate(flops=10**9, bytes_accessed=2 * 10**6, transcendentals=0),
        name="slot_sums",
    )(block_terms, operators, core_tensor)


def exchange(array, axes, flip):
    count = lax.axis_size(axes)
    return lax.ppermute(array, axes, [(i, i ^ flip) for i in range(count)])


def scatter_sum(array, axes, place, flips):
    rows = array.shape[0] // (len(flips) + 1)

    def block(index):
        return lax.dynamic_slice_in_dim(array, index * rows, rows, 0)

    arrived = [exchange(block(place ^ own), axes, flip) for flip, own in flips]
    total = block(place).astype(F32)
    for part in arrived:
        total = total + part.astype(F32)
    return total.astype(BF)


def gather_blocks(array, axes, place, flips):
    rows = array.shape[0]
    whole = jnp.zeros((rows * (len(flips) + 1),) + array.shape[1:], array.dtype)
    arrived = [(own, exchange(array, axes, flip)) for flip, own in flips]
    whole = lax.dynamic_update_slice_in_dim(whole, array, place * rows, 0)
    for own, part in arrived:
        whole = lax.dynamic_update_slice_in_dim(whole, part, (place ^ own) * rows, 0)
    return whole


def bit_flips(bits):
    flips = []
    for own in range(1, 1 << len(bits)):
        flip = sum(1 << bit for at, bit in enumerate(bits) if own >> at & 1)
        flips.append((flip, own))
    return flips


def place_of(index, bits):
    place = jnp.int32(0)
    for at, bit in enumerate(bits):
        place = place | (((index >> bit) & 1) << at)
    return place


def total_mean_fields(partial, potential):
    terms, width_a, width = partial.shape
    group_index = lax.axis_index(GROUP)
    tile_index = lax.axis_index("tile")
    tile_bits = list(range(lax.axis_size("tile").bit_length() - 1))
    group_bits = list(range(lax.axis_size(GROUP).bit_length() - 1))
    far = lax.axis_size("grp").bit_length() - 2
    near = [bit for bit in group_bits if bit != far]
    stages = [("tile", tile_index, tile_bits), (GROUP, group_index, near)]
    array = partial.reshape(terms * width_a, width)
    for axes, index, bits in stages:
        array = scatter_sum(array, axes, place_of(index, bits), bit_flips(bits))
    array = (array.astype(F32) + exchange(array, GROUP, 1 << far).astype(F32)).astype(BF)
    for axes, index, bits in reversed(stages):
        array = gather_blocks(array, axes, place_of(index, bits), bit_flips(bits))
        array, potential = lax.optimization_barrier((array, potential))
    return array.reshape(terms, width_a, width), potential


def action_kernel(points_ref, weight_ref, mean_ref, out_ref, blocks):
    width_a = mean_ref.shape[1]
    rows, width = points_ref.shape
    width_b = width - width_a

    @pl.when(pl.program_id(0) == 0)
    def _():
        lane = lax.broadcasted_iota(jnp.int32, (width_a, width), 1)
        for term in range(TERMS):
            packed = mean_ref[term].astype(F32)
            blocks[term, :width_a, :] = jnp.where(lane < width_a, packed, 0.0).astype(BF)
            blocks[term, width_a:, :] = jnp.where(
                lane[:width_b] < width_a, 0.0, packed[:width_b]
            ).astype(BF)

    step = 256
    for start in range(0, rows, step):
        points = points_ref[start : start + step, :]
        on_a = lax.broadcasted_iota(jnp.int32, (step, width), 1) < width_a
        scaled = []
        for term in range(TERMS):
            weight_a = weight_ref[start : start + step, term : term + 1]
            weight_b = weight_ref[start : start + step, TERMS + term : TERMS + term + 1]
            scaled.append(points * jnp.where(on_a, weight_a, weight_b))
        out_ref[start : start + step, :] = jnp.dot(
            jnp.concatenate(scaled, axis=1),
            blocks[...].reshape(TERMS * width, width),
            preferred_element_type=F32,
        )


def action_of(orbitals, potential, mean):
    rows_x, rows_y, width = orbitals.shape
    count = rows_x * rows_y
    points = orbitals.reshape(count, width)
    weights = potential.reshape(2 * TERMS, count).T.astype(BF)
    step = 512
    action = pl.pallas_call(
        action_kernel,
        grid=(count // step,),
        out_shape=jax.ShapeDtypeStruct((count, width), F32),
        in_specs=[
            pl.BlockSpec((step, width), lambda i: (i, 0)),
            pl.BlockSpec((step, 2 * TERMS), lambda i: (i, 0)),
            pl.BlockSpec(mean.shape, lambda i: (0, 0, 0)),
        ],
        out_specs=pl.BlockSpec((step, width), lambda i: (i, 0)),
        scratch_shapes=[pltpu.VMEM((TERMS, width, width), BF)],
        cost_estimate=pl.CostEstimate(
            flops=2 * count * width * width * TERMS, bytes_accessed=2 * 10**7, transcendentals=0
        ),
        name="action",
    )(points, weights, mean)
    return action.reshape(rows_x, rows_y, width)


def split_kernel(groups, me_ref, orb_ref, *refs):
    outs, rows = refs[:groups], refs[groups]
    step_x, side, width = orb_ref.shape
    per = side // groups
    swap = swap_matrix()
    for start in range(0, step_x, SIDE):
        block = orb_ref[start : start + SIDE].reshape(SIDE * SIDE, width)
        turned = jnp.dot(swap, block, preferred_element_type=F32).astype(BF)
        rows[:, start : start + SIDE, :] = turned.reshape(SIDE, SIDE, width)
    me = me_ref[0]
    for flip in range(groups):
        outs[flip][...] = rows[pl.ds((me ^ flip) * per, per)]


def split_chunk(me, orbitals, first_row, chunk, groups):
    rows_x, _, width = orbitals.shape
    first, per, step_x = first_row // SIDE, SIDE // groups, rows_x // 2
    return pl.pallas_call(
        functools.partial(split_kernel, groups),
        grid=(chunk // SIDE, rows_x // step_x),
        out_shape=[jax.ShapeDtypeStruct((chunk // groups, rows_x, width), BF)] * groups,
        in_specs=[SMEM, pl.BlockSpec((step_x, SIDE, width), lambda p, i: (i, first + p, 0))],
        out_specs=[pl.BlockSpec((per, step_x, width), lambda p, i: (p, i, 0))] * groups,
        scratch_shapes=[pltpu.VMEM((SIDE, step_x, width), BF)],
        cost_estimate=pl.CostEstimate(
            flops=2 * rows_x * chunk * width * SIDE * SIDE,
            bytes_accessed=4 * rows_x * chunk * width,
            transcendentals=0,
        ),
        name="split",
    )(me, orbitals)


def apply_kernel(groups, me_ref, kin_ref, *refs):
    pieces, outs = refs[:groups], refs[groups : 2 * groups]
    gathered, result = refs[2 * groups :]
    _, rows_x, _ = pieces[0].shape
    size_x = kin_ref.shape[0]
    me = me_ref[0]
    for flip in range(groups):
        start = pl.multiple_of((me ^ flip) * rows_x, rows_x)
        gathered[pl.ds(start, rows_x), :] = pieces[flip][0]
    step = 512
    for start in range(0, size_x, step):
        applied = jnp.dot(
            kin_ref[start : start + step, :], gathered[...], preferred_element_type=F32
        )
        result[start : start + step, :] = applied.astype(BF)
    for flip in range(groups):
        start = pl.multiple_of((me ^ flip) * rows_x, rows_x)
        outs[flip][0] = result[pl.ds(start, rows_x), :]


def apply_chunk(me, kinetic, pieces):
    groups = len(pieces)
    per, rows_x, width = pieces[0].shape
    size_x = kinetic.shape[0]
    block = pl.BlockSpec((1, rows_x, width), lambda i: (i, 0, 0))
    whole = pl.BlockSpec((size_x, size_x), lambda i: (0, 0), pipeline_mode=pl.Buffered(1))
    return pl.pallas_call(
        functools.partial(apply_kernel, groups),
        grid=(per,),
        out_shape=[jax.ShapeDtypeStruct((per, rows_x, width), BF)] * groups,
        in_specs=[SMEM, whole] + [block] * groups,
        out_specs=[block] * groups,
        scratch_shapes=[pltpu.VMEM((size_x, width), BF)] * 2,
        cost_estimate=pl.CostEstimate(
            flops=2 * size_x * size_x * per * width, bytes_accessed=4 * 10**6, transcendentals=0
        ),
        name="apply",
    )(me, kinetic, *pieces)


def join_kernel(groups, me_ref, action_ref, *refs):
    pieces = refs[:groups]
    out_ref, rows = refs[-2:]
    per = pieces[0].shape[0]
    step_x, _, width = out_ref.shape
    me = me_ref[0]
    for flip in range(groups):
        rows[pl.ds((me ^ flip) * per, per)] = pieces[flip][...]
    swap = swap_matrix()
    for start in range(0, step_x, SIDE):
        block = rows[:, start : start + SIDE, :].reshape(SIDE * SIDE, width)
        turned = jnp.dot(swap, block, preferred_element_type=F32).reshape(SIDE, SIDE, width)
        out_ref[start : start + SIDE] = (turned + action_ref[start : start + SIDE]).astype(BF)


def join_chunk(me, action, pieces, first_row, before):
    groups = len(pieces)
    _, rows_x, width = pieces[0].shape
    chunk = pieces[0].shape[0] * groups
    rows_y = action.shape[1]
    first, per, step_x = first_row // SIDE, SIDE // groups, rows_x // 2
    block = pl.BlockSpec((step_x, SIDE, width), lambda p, i: (i, first + p, 0))
    in_specs = [SMEM, block] + [pl.BlockSpec((per, step_x, width), lambda p, i: (p, i, 0))] * groups
    operands = [me, action, *pieces]
    aliases = {}
    if before is not None:
        in_specs.append(pl.BlockSpec(memory_space=pl.ANY))
        aliases = {len(operands): 0}
        operands.append(before)
    return pl.pallas_call(
        functools.partial(join_kernel, groups),
        grid=(chunk // SIDE, rows_x // step_x),
        out_shape=jax.ShapeDtypeStruct((rows_x, rows_y, width), BF),
        in_specs=in_specs,
        out_specs=block,
        scratch_shapes=[pltpu.VMEM((SIDE, step_x, width), BF)],
        input_output_aliases=aliases,
        cost_estimate=pl.CostEstimate(
            flops=2 * rows_x * chunk * width * SIDE * SIDE,
            bytes_accessed=8 * rows_x * chunk * width,
            transcendentals=0,
        ),
        name="join",
    )(*operands)


def exchange_all(pieces):
    groups = len(pieces)
    far = lax.axis_size("grp") // 2
    order = sorted(range(1, groups), key=lambda flip: (flip & far == 0, flip))
    arrived = list(pieces)
    for flip in order:
        arrived[flip] = exchange(pieces[flip], GROUP, flip)
    return arrived


def chunk_sizes(rows_y):
    if rows_y < 3 * SIDE:
        return [SIDE] * (rows_y // SIDE)
    return [rows_y - 2 * SIDE, SIDE, SIDE]


def chunked_body(core_tensor, term_operators, block_terms, orbitals, potential, kinetic):
    _, rows_y, _ = orbitals.shape
    groups = lax.axis_size(GROUP)
    sizes = chunk_sizes(rows_y)
    first_rows = [sum(sizes[:index]) for index in range(len(sizes))]
    me = lax.axis_index(GROUP).astype(jnp.int32).reshape(1)
    returned = []
    for first, size in zip(first_rows, sizes):
        pieces = split_chunk(me, orbitals, first, size, groups)
        pieces = exchange_all(pieces)
        pieces = apply_chunk(me, kinetic, pieces)
        returned.append(exchange_all(pieces))
    partial = tile_mean_fields(core_tensor, term_operators, block_terms)
    mean, potential = total_mean_fields(partial, potential)
    action = action_of(orbitals, potential, mean)
    result = None
    for index, first in enumerate(first_rows):
        result = join_chunk(me, action, returned[index], first, result)
    return result


def fits(core_tensor, orbitals, mesh):
    rows_x, rows_y, width = orbitals
    groups = mesh.shape["half"] * mesh.shape["grp"]
    tiles = mesh.shape["tile"]
    _, width_b, width_a = core_tensor
    return (
        mesh.shape["half"] == 2
        and mesh.shape["grp"] >= 2
        and groups & (groups - 1) == 0
        and tiles & (tiles - 1) == 0
        and tiles > 1
        and SIDE % groups == 0
        and rows_y % SIDE == 0
        and rows_x % 128 == 0
        and width == width_a + width_b
        and width % 256 == 0
        and width_b % 16 == 0
        and width_a % 16 == 0
        and width_b <= width_a
        and TERMS * width_a % (groups * tiles * 8) == 0
    )


def solution(mesh):
    specs = (
        P(("half", "grp", "tile"), None, None),
        P(("half", "grp", "tile"), None, None, None),
        P(("half", "grp", "tile"), None),
        P(("half", "grp"), "tile", None),
        P(None, None, ("half", "grp"), "tile"),
        P(),
    )

    def build(body):
        return jax.shard_map(body, mesh=mesh, in_specs=specs, out_specs=specs[3], check_vma=False)

    def whole(core_tensor, term_operators, block_terms, orbitals, potential, kinetic):
        args = (core_tensor, term_operators, block_terms, orbitals, potential, kinetic)
        size_x, size_y, width = orbitals.shape
        rows_x = size_x // (mesh.shape["half"] * mesh.shape["grp"])
        rows_y = size_y // mesh.shape["tile"]
        if not fits(core_tensor.shape, (rows_x, rows_y, width), mesh):
            return build(plain_body)(*args)
        return build(chunked_body)(*args)

    return whole
```

```python
import functools
from typing import NamedTuple

import jax
import jax.numpy as jnp
from jax import lax
from jax.experimental import pallas as pl
from jax.experimental.pallas import tpu as pltpu
from jax.sharding import PartitionSpec as P


TERMS = 8
GROUP = ("half", "grp")
LANES = 256
BF = jnp.bfloat16
F32 = jnp.float32


def slot_sums(core_tensor, term_operators, block_terms):
    rows_tile, width_b, width_a = core_tensor.shape
    flat_core = core_tensor.reshape(rows_tile, width_b * width_a)
    listed = block_terms[0]
    live_slots = jnp.sum((listed < TERMS).astype(jnp.int32))
    labels = jnp.arange(TERMS, dtype=jnp.int32)

    def add_slot(slot_index, running):
        sum_a, sum_b = running
        operator = term_operators[0, slot_index]
        mixed_core = jnp.einsum("rs,rq->sq", operator, flat_core, preferred_element_type=F32)
        mixed_core = mixed_core.astype(BF).reshape(rows_tile, width_b, width_a)
        gram_a = jnp.einsum("rba,rbc->ac", core_tensor, mixed_core, preferred_element_type=F32)
        gram_b = jnp.einsum("rba,rda->bd", core_tensor, mixed_core, preferred_element_type=F32)
        chosen = (labels == listed[slot_index]).astype(F32)
        return (sum_a + chosen[:, None, None] * gram_a, sum_b + chosen[:, None, None] * gram_b)

    start_sums = (
        jnp.zeros((TERMS, width_a, width_a), F32),
        jnp.zeros((TERMS, width_b, width_b), F32),
    )
    return lax.fori_loop(0, live_slots, add_slot, start_sums)


def point_action(points, weights, stack_a, stack_b):
    width_a = stack_a.shape[0]
    width_b = stack_b.shape[0]
    count_points = points.shape[0]
    prod_a = jnp.dot(points[:, :width_a], stack_a, preferred_element_type=F32).reshape(
        count_points, TERMS, width_a
    )
    prod_b = jnp.dot(points[:, width_a:], stack_b, preferred_element_type=F32).reshape(
        count_points, TERMS, width_b
    )
    act_a = jnp.sum(prod_a * weights[0].T[:, :, None], axis=1)
    act_b = jnp.sum(prod_b * weights[1].T[:, :, None], axis=1)
    return jnp.concatenate([act_a, act_b], axis=1)


def kinetic_columns(kinetic, orbitals):
    rows_x, rows_y, width_all = orbitals.shape
    groups = lax.axis_size("half") * lax.axis_size("grp")
    columns = rows_y * width_all // groups
    pieces = orbitals.reshape(rows_x, groups, columns)
    applied = jnp.einsum(
        "xz,zik->xik",
        kinetic,
        lax.all_to_all(pieces, GROUP, split_axis=1, concat_axis=0, tiled=True),
        preferred_element_type=F32,
    )
    applied = applied.astype(BF)
    returned = lax.all_to_all(applied, GROUP, split_axis=0, concat_axis=1, tiled=True)
    return returned.reshape(rows_x, rows_y, width_all)


def plain_body(core_tensor, term_operators, block_terms, orbitals, potential, kinetic):
    sum_a, sum_b = slot_sums(core_tensor, term_operators, block_terms)
    total_a, total_b = lax.psum((sum_a, sum_b), ("half", "grp", "tile"))
    mean_a = total_a.astype(BF)
    mean_b = total_b.astype(BF)
    kinetic_part = kinetic_columns(kinetic, orbitals)
    rows_x, rows_y, width_all = orbitals.shape
    width_a = mean_a.shape[1]
    width_b = mean_b.shape[1]
    stack_a = jnp.transpose(mean_a, (1, 0, 2)).reshape(width_a, TERMS * width_a)
    stack_b = jnp.transpose(mean_b, (1, 0, 2)).reshape(width_b, TERMS * width_b)
    points = orbitals.reshape(rows_x * rows_y, width_all)
    weights = potential.reshape(2, TERMS, rows_x * rows_y)
    action = point_action(points, weights, stack_a, stack_b).reshape(rows_x, rows_y, width_all)
    return (kinetic_part.astype(F32) + action).astype(BF)


VMEM = pl.BlockSpec(memory_space=pltpu.VMEM)
SMEM = pl.BlockSpec(memory_space=pltpu.SMEM)


def place_matrix(me, flips, side, turned):
    groups = side.groups
    per, step = side.rows // groups, side.points
    count = len(flips) * per * step
    shape = (step * side.rows, count) if turned else (count, step * side.rows)
    to = lax.broadcasted_iota(jnp.int32, shape, 1 if turned else 0)
    source = lax.broadcasted_iota(jnp.int32, shape, 0 if turned else 1)
    flip = jnp.zeros(shape, jnp.int32)
    for at, value in enumerate(flips):
        flip = jnp.where(to // (per * step) == at, value, flip)
    wanted = (to % step) * side.rows + (me ^ flip) * per + (to // step) % per
    return jnp.where(wanted == source, 1.0, 0.0).astype(BF)


def slot_kernel(terms_ref, oper_ref, core_ref, out_ref, core_f, core_t, core_p, mixed):
    rows, width_b, width_a = core_ref.shape
    width = out_ref.shape[2]
    slots = terms_ref.shape[1]
    out_ref[...] = jnp.zeros_like(out_ref)
    mixed[...] = jnp.zeros_like(mixed)
    core_p[...] = jnp.zeros_like(core_p)
    core_p[:, :, :width_a] = core_ref[...]
    core_f[...] = core_p[...].astype(F32)
    core_t[...] = jnp.transpose(core_f[...].reshape(rows * width_b, width)).astype(BF)
    live = jnp.int32(0)
    for slot in range(slots):
        live = live + (terms_ref[0, slot] < TERMS).astype(jnp.int32)

    def one_slot(slot, carry):
        def one_block(block, inner):
            start = pl.multiple_of(block * 16, 16)
            source = [core_f[r, pl.ds(start, 16), :] for r in range(rows)]
            for q in range(rows):
                total = source[0] * oper_ref[slot, q]
                for r in range(1, rows):
                    total = total + source[r] * oper_ref[slot, r * rows + q]
                mixed[q, pl.ds(width_a + start, 16), :] = total.astype(BF)
            return inner

        lax.fori_loop(0, width_b // 16, one_block, 0)
        flat = mixed[:, width_a:, :].reshape(rows * width_b, width)
        gram_a = jnp.dot(core_t[:width_a, :], flat, preferred_element_type=F32)
        gram_b = jnp.zeros((width_b, width), F32)
        for q in range(rows):
            gram_b = gram_b + lax.dot_general(
                core_p[q], mixed[q], (((1,), (1,)), ((), ())), preferred_element_type=F32
            )
        term = terms_ref[0, slot]
        out_ref[term, :width_b, :] = (gram_a[:width_b] + gram_b).astype(BF)
        out_ref[term, width_b:, :] = gram_a[width_b:].astype(BF)
        return carry

    lax.fori_loop(0, live, one_slot, 0)


def tile_mean_fields(core_tensor, term_operators, block_terms):
    rows, width_b, width_a = core_tensor.shape
    slots = block_terms.shape[1]
    width = width_a + width_b
    operators = term_operators.astype(F32).reshape(slots, rows * rows)
    return pl.pallas_call(
        slot_kernel,
        out_shape=jax.ShapeDtypeStruct((TERMS, width_a, width), BF),
        in_specs=[SMEM, SMEM, VMEM],
        out_specs=VMEM,
        scratch_shapes=[
            pltpu.VMEM((rows, width_b, width), F32),
            pltpu.VMEM((width, rows * width_b), BF),
            pltpu.VMEM((rows, width_b, width), BF),
            pltpu.VMEM((rows, width, width), BF),
        ],
        cost_estimate=pl.CostEstimate(flops=10**9, bytes_accessed=2 * 10**6, transcendentals=0),
        name="slot_sums",
    )(block_terms, operators, core_tensor)


def exchange(array, axes, flip):
    count = lax.axis_size(axes)
    return lax.ppermute(array, axes, [(i, i ^ flip) for i in range(count)])


def scatter_sum(array, axes, place, flips):
    rows = array.shape[0] // (len(flips) + 1)

    def block(index):
        return lax.dynamic_slice_in_dim(array, index * rows, rows, 0)

    arrived = [exchange(block(place ^ own), axes, flip) for flip, own in flips]
    total = block(place).astype(F32)
    for part in arrived:
        total = total + part.astype(F32)
    return total.astype(BF)


def gather_blocks(array, axes, place, flips):
    rows = array.shape[0]
    whole = jnp.zeros((rows * (len(flips) + 1),) + array.shape[1:], array.dtype)
    arrived = [(own, exchange(array, axes, flip)) for flip, own in flips]
    whole = lax.dynamic_update_slice_in_dim(whole, array, place * rows, 0)
    for own, part in arrived:
        whole = lax.dynamic_update_slice_in_dim(whole, part, (place ^ own) * rows, 0)
    return whole


def bit_flips(bits):
    flips = []
    for own in range(1, 1 << len(bits)):
        flip = sum(1 << bit for at, bit in enumerate(bits) if own >> at & 1)
        flips.append((flip, own))
    return flips


def place_of(index, bits):
    place = jnp.int32(0)
    for at, bit in enumerate(bits):
        place = place | (((index >> bit) & 1) << at)
    return place


def total_mean_fields(partial, potential):
    terms, width_a, width = partial.shape
    group_index = lax.axis_index(GROUP)
    tile_index = lax.axis_index("tile")
    tile_bits = list(range(lax.axis_size("tile").bit_length() - 1))
    group_bits = list(range(lax.axis_size(GROUP).bit_length() - 1))
    far = lax.axis_size("grp").bit_length() - 2
    near = [bit for bit in group_bits if bit != far]
    stages = [("tile", tile_index, tile_bits), (GROUP, group_index, near)]
    array = partial.reshape(terms * width_a, width)
    for axes, index, bits in stages:
        array = scatter_sum(array, axes, place_of(index, bits), bit_flips(bits))
    array = (array.astype(F32) + exchange(array, GROUP, 1 << far).astype(F32)).astype(BF)
    for axes, index, bits in reversed(stages):
        array = gather_blocks(array, axes, place_of(index, bits), bit_flips(bits))
        array, potential = lax.optimization_barrier((array, potential))
    return array.reshape(terms, width_a, width), potential


def action_kernel(points_ref, weight_ref, mean_ref, out_ref, blocks):
    width_a = mean_ref.shape[1]
    rows, width = points_ref.shape
    width_b = width - width_a

    @pl.when(pl.program_id(0) == 0)
    def _():
        lane = lax.broadcasted_iota(jnp.int32, (width_a, width), 1)
        for term in range(TERMS):
            packed = mean_ref[term].astype(F32)
            blocks[term, :width_a, :] = jnp.where(lane < width_a, packed, 0.0).astype(BF)
            blocks[term, width_a:, :] = jnp.where(
                lane[:width_b] < width_a, 0.0, packed[:width_b]
            ).astype(BF)

    step = 256
    for start in range(0, rows, step):
        points = points_ref[start : start + step, :]
        on_a = lax.broadcasted_iota(jnp.int32, (step, width), 1) < width_a
        scaled = []
        for term in range(TERMS):
            weight_a = weight_ref[start : start + step, term : term + 1]
            weight_b = weight_ref[start : start + step, TERMS + term : TERMS + term + 1]
            scaled.append(points * jnp.where(on_a, weight_a, weight_b))
        out_ref[start : start + step, :] = jnp.dot(
            jnp.concatenate(scaled, axis=1),
            blocks[...].reshape(TERMS * width, width),
            preferred_element_type=F32,
        )


def action_of(orbitals, potential, mean):
    rows_x, rows_y, width = orbitals.shape
    count = rows_x * rows_y
    points = orbitals.reshape(count, width)
    weights = potential.reshape(2 * TERMS, count).T.astype(BF)
    step = 512
    action = pl.pallas_call(
        action_kernel,
        grid=(count // step,),
        out_shape=jax.ShapeDtypeStruct((count, width), F32),
        in_specs=[
            pl.BlockSpec((step, width), lambda i: (i, 0)),
            pl.BlockSpec((step, 2 * TERMS), lambda i: (i, 0)),
            pl.BlockSpec(mean.shape, lambda i: (0, 0, 0)),
        ],
        out_specs=pl.BlockSpec((step, width), lambda i: (i, 0)),
        scratch_shapes=[pltpu.VMEM((TERMS, width, width), BF)],
        cost_estimate=pl.CostEstimate(
            flops=2 * count * width * width * TERMS, bytes_accessed=2 * 10**7, transcendentals=0
        ),
        name="action",
    )(points, weights, mean)
    return action.reshape(rows_x, rows_y, width)


class Side(NamedTuple):
    groups: int
    rows: int
    points: int


def side_of(groups):
    rows = max(8, groups)
    return Side(groups, rows, LANES // rows)


def block_rows(first_row, chunk, side):
    rows = side.rows
    while chunk % (2 * rows) == 0 and first_row % (2 * rows) == 0 and rows < 32:
        rows *= 2
    return rows


def split_kernel(flips, side, me_ref, orb_ref, *refs):
    outs, matrix = refs[:-1], refs[-1]
    rows_x, rows, width = orb_ref.shape
    per, step = side.rows // side.groups, side.points

    @pl.when(pl.program_id(0) == 0)
    def _():
        matrix[...] = place_matrix(me_ref[0], flips, side, False)

    for part in range(rows // side.rows):
        for start in range(0, rows_x, step):
            block = orb_ref[start : start + step, part * side.rows : (part + 1) * side.rows, :]
            moved = jnp.dot(
                matrix[...], block.reshape(step * side.rows, width), preferred_element_type=F32
            )
            moved = moved.astype(BF).reshape(len(flips), per, step, width)
            for at in range(len(flips)):
                outs[at][part * per : (part + 1) * per, start : start + step, :] = moved[at]


def split_chunk(me, orbitals, first_row, chunk, flips, side):
    rows_x, _, width = orbitals.shape
    rows = block_rows(first_row, chunk, side)
    piece = (rows // side.groups, rows_x, width)
    return pl.pallas_call(
        functools.partial(split_kernel, tuple(flips), side),
        grid=(chunk // rows,),
        out_shape=[jax.ShapeDtypeStruct((chunk // side.groups, rows_x, width), BF)] * len(flips),
        in_specs=[
            SMEM,
            pl.BlockSpec((rows_x, rows, width), lambda p: (0, first_row // rows + p, 0)),
        ],
        out_specs=[pl.BlockSpec(piece, lambda p: (p, 0, 0))] * len(flips),
        scratch_shapes=[pltpu.VMEM((len(flips) * LANES // side.groups, LANES), BF)],
        cost_estimate=pl.CostEstimate(
            flops=2 * rows_x * chunk * width * LANES,
            bytes_accessed=4 * rows_x * chunk * width,
            transcendentals=0,
        ),
        name="split",
    )(me, orbitals)


def apply_kernel(groups, me_ref, kin_ref, *refs):
    pieces, outs = refs[:groups], refs[groups : 2 * groups]
    gathered, result = refs[2 * groups :]
    _, rows_x, _ = pieces[0].shape
    size_x = kin_ref.shape[0]
    me = me_ref[0]
    for flip in range(groups):
        start = pl.multiple_of((me ^ flip) * rows_x, rows_x)
        gathered[pl.ds(start, rows_x), :] = pieces[flip][0]
    step = 512
    for start in range(0, size_x, step):
        applied = jnp.dot(
            kin_ref[start : start + step, :], gathered[...], preferred_element_type=F32
        )
        result[start : start + step, :] = applied.astype(BF)
    for flip in range(groups):
        start = pl.multiple_of((me ^ flip) * rows_x, rows_x)
        outs[flip][0] = result[pl.ds(start, rows_x), :]


def apply_chunk(me, kinetic, pieces):
    groups = len(pieces)
    per, rows_x, width = pieces[0].shape
    size_x = kinetic.shape[0]
    block = pl.BlockSpec((1, rows_x, width), lambda i: (i, 0, 0))
    whole = pl.BlockSpec((size_x, size_x), lambda i: (0, 0), pipeline_mode=pl.Buffered(1))
    return pl.pallas_call(
        functools.partial(apply_kernel, groups),
        grid=(per,),
        out_shape=[jax.ShapeDtypeStruct((per, rows_x, width), BF)] * groups,
        in_specs=[SMEM, whole] + [block] * groups,
        out_specs=[block] * groups,
        scratch_shapes=[pltpu.VMEM((size_x, width), BF)] * 2,
        cost_estimate=pl.CostEstimate(
            flops=2 * size_x * size_x * per * width, bytes_accessed=4 * 10**6, transcendentals=0
        ),
        name="apply",
    )(me, kinetic, *pieces)


def join_kernel(side, me_ref, action_ref, *refs):
    pieces = refs[: side.groups]
    out_ref, matrix = refs[-2:]
    step_x, rows, width = out_ref.shape
    per, step = side.rows // side.groups, side.points

    @pl.when((pl.program_id(0) == 0) & (pl.program_id(1) == 0))
    def _():
        matrix[...] = place_matrix(me_ref[0], range(side.groups), side, True)

    for part in range(rows // side.rows):
        here = slice(part * side.rows, (part + 1) * side.rows)
        for start in range(0, step_x, step):
            block = jnp.concatenate(
                [
                    piece[part * per : (part + 1) * per, start : start + step, :]
                    for piece in pieces
                ],
                axis=0,
            ).reshape(step * side.rows, width)
            moved = jnp.dot(matrix[...], block, preferred_element_type=F32)
            total = moved.reshape(step, side.rows, width) + action_ref[start : start + step, here, :]
            out_ref[start : start + step, here, :] = total.astype(BF)


def join_chunk(me, action, pieces, first_row, before, side):
    groups = len(pieces)
    _, rows_x, width = pieces[0].shape
    chunk = pieces[0].shape[0] * groups
    rows_y = action.shape[1]
    rows = block_rows(first_row, chunk, side)
    step_x = rows_x // 2 if chunk == rows else rows_x
    block = pl.BlockSpec((step_x, rows, width), lambda p, i: (i, first_row // rows + p, 0))
    piece = pl.BlockSpec((rows // groups, step_x, width), lambda p, i: (p, i, 0))
    in_specs = [SMEM, block] + [piece] * groups
    operands = [me, action, *pieces]
    aliases = {}
    if before is not None:
        in_specs.append(pl.BlockSpec(memory_space=pl.ANY))
        aliases = {len(operands): 0}
        operands.append(before)
    return pl.pallas_call(
        functools.partial(join_kernel, side),
        grid=(chunk // rows, rows_x // step_x),
        out_shape=jax.ShapeDtypeStruct((rows_x, rows_y, width), BF),
        in_specs=in_specs,
        out_specs=block,
        scratch_shapes=[pltpu.VMEM((LANES, LANES), BF)],
        input_output_aliases=aliases,
        cost_estimate=pl.CostEstimate(
            flops=2 * rows_x * chunk * width * LANES,
            bytes_accessed=8 * rows_x * chunk * width,
            transcendentals=0,
        ),
        name="join",
    )(*operands)


def far_flip():
    return lax.axis_size("grp") // 2


def exchange_some(pieces, flips):
    return {flip: exchange(pieces[flip], GROUP, flip) if flip else pieces[0] for flip in flips}


def exchange_all(pieces, near_first):
    far = far_flip()
    order = sorted(range(len(pieces)), key=lambda flip: (bool(flip & far) == near_first, flip))
    arrived = exchange_some(pieces, order)
    return [arrived[flip] for flip in range(len(pieces))]


def chunk_sizes(rows_y, side):
    if rows_y % (4 * side.rows):
        return [side.rows] * (rows_y // side.rows)
    return [rows_y // 2, rows_y // 4, rows_y // 4]


def chunked_body(core_tensor, term_operators, block_terms, orbitals, potential, kinetic):
    _, rows_y, _ = orbitals.shape
    groups = lax.axis_size(GROUP)
    side = side_of(groups)
    sizes = chunk_sizes(rows_y, side)
    first_rows = [sum(sizes[:index]) for index in range(len(sizes))]
    far = [flip for flip in range(groups) if flip & far_flip()]
    near = [flip for flip in range(groups) if flip not in far]
    me = lax.axis_index(GROUP).astype(jnp.int32).reshape(1)
    returned = []
    for index, (first, size) in enumerate(zip(first_rows, sizes)):
        if index == 0:
            arrived = {}
            for flips in (far, near):
                cut = split_chunk(me, orbitals, first, size, flips, side)
                arrived.update(exchange_some(dict(zip(flips, cut)), flips))
            pieces = [arrived[flip] for flip in range(groups)]
        else:
            pieces = split_chunk(me, orbitals, first, size, range(groups), side)
            pieces = exchange_all(pieces, True)
        pieces = apply_chunk(me, kinetic, pieces)
        returned.append(exchange_all(pieces, True))
    partial = tile_mean_fields(core_tensor, term_operators, block_terms)
    mean, potential = total_mean_fields(partial, potential)
    action = action_of(orbitals, potential, mean)
    result = None
    for index, first in enumerate(first_rows):
        result = join_chunk(me, action, returned[index], first, result, side)
    return result


def fits(core_tensor, orbitals, mesh):
    rows_x, rows_y, width = orbitals
    groups = mesh.shape["half"] * mesh.shape["grp"]
    tiles = mesh.shape["tile"]
    _, width_b, width_a = core_tensor
    return (
        mesh.shape["half"] == 2
        and mesh.shape["grp"] >= 2
        and groups & (groups - 1) == 0
        and tiles & (tiles - 1) == 0
        and tiles > 1
        and groups % 8 == 0
        and LANES % (2 * groups) == 0
        and rows_y % groups == 0
        and rows_x % 128 == 0
        and width == width_a + width_b
        and width % 256 == 0
        and width_b % 16 == 0
        and width_a % 16 == 0
        and width_b <= width_a
        and TERMS * width_a % (groups * tiles * 8) == 0
    )


def solution(mesh):
    specs = (
        P(("half", "grp", "tile"), None, None),
        P(("half", "grp", "tile"), None, None, None),
        P(("half", "grp", "tile"), None),
        P(("half", "grp"), "tile", None),
        P(None, None, ("half", "grp"), "tile"),
        P(),
    )

    def build(body):
        return jax.shard_map(body, mesh=mesh, in_specs=specs, out_specs=specs[3], check_vma=False)

    def whole(core_tensor, term_operators, block_terms, orbitals, potential, kinetic):
        args = (core_tensor, term_operators, block_terms, orbitals, potential, kinetic)
        size_x, size_y, width = orbitals.shape
        rows_x = size_x // (mesh.shape["half"] * mesh.shape["grp"])
        rows_y = size_y // mesh.shape["tile"]
        if not fits(core_tensor.shape, (rows_x, rows_y, width), mesh):
            return build(plain_body)(*args)
        return build(chunked_body)(*args)

    return whole
```

```python
import functools
from typing import NamedTuple

import jax
import jax.numpy as jnp
from jax import lax
from jax.experimental import pallas as pl
from jax.experimental.pallas import tpu as pltpu
from jax.sharding import PartitionSpec as P


TERMS = 8
GROUP = ("half", "grp")
LANES = 256
BF = jnp.bfloat16
F32 = jnp.float32


def slot_sums(core_tensor, term_operators, block_terms):
    rows_tile, width_b, width_a = core_tensor.shape
    flat_core = core_tensor.reshape(rows_tile, width_b * width_a)
    listed = block_terms[0]
    live_slots = jnp.sum((listed < TERMS).astype(jnp.int32))
    labels = jnp.arange(TERMS, dtype=jnp.int32)

    def add_slot(slot_index, running):
        sum_a, sum_b = running
        operator = term_operators[0, slot_index]
        mixed_core = jnp.einsum("rs,rq->sq", operator, flat_core, preferred_element_type=F32)
        mixed_core = mixed_core.astype(BF).reshape(rows_tile, width_b, width_a)
        gram_a = jnp.einsum("rba,rbc->ac", core_tensor, mixed_core, preferred_element_type=F32)
        gram_b = jnp.einsum("rba,rda->bd", core_tensor, mixed_core, preferred_element_type=F32)
        chosen = (labels == listed[slot_index]).astype(F32)
        return (sum_a + chosen[:, None, None] * gram_a, sum_b + chosen[:, None, None] * gram_b)

    start_sums = (
        jnp.zeros((TERMS, width_a, width_a), F32),
        jnp.zeros((TERMS, width_b, width_b), F32),
    )
    return lax.fori_loop(0, live_slots, add_slot, start_sums)


def point_action(points, weights, stack_a, stack_b):
    width_a = stack_a.shape[0]
    width_b = stack_b.shape[0]
    count_points = points.shape[0]
    prod_a = jnp.dot(points[:, :width_a], stack_a, preferred_element_type=F32).reshape(
        count_points, TERMS, width_a
    )
    prod_b = jnp.dot(points[:, width_a:], stack_b, preferred_element_type=F32).reshape(
        count_points, TERMS, width_b
    )
    act_a = jnp.sum(prod_a * weights[0].T[:, :, None], axis=1)
    act_b = jnp.sum(prod_b * weights[1].T[:, :, None], axis=1)
    return jnp.concatenate([act_a, act_b], axis=1)


def kinetic_columns(kinetic, orbitals):
    rows_x, rows_y, width_all = orbitals.shape
    groups = lax.axis_size("half") * lax.axis_size("grp")
    columns = rows_y * width_all // groups
    pieces = orbitals.reshape(rows_x, groups, columns)
    applied = jnp.einsum(
        "xz,zik->xik",
        kinetic,
        lax.all_to_all(pieces, GROUP, split_axis=1, concat_axis=0, tiled=True),
        preferred_element_type=F32,
    )
    applied = applied.astype(BF)
    returned = lax.all_to_all(applied, GROUP, split_axis=0, concat_axis=1, tiled=True)
    return returned.reshape(rows_x, rows_y, width_all)


def plain_body(core_tensor, term_operators, block_terms, orbitals, potential, kinetic):
    sum_a, sum_b = slot_sums(core_tensor, term_operators, block_terms)
    total_a, total_b = lax.psum((sum_a, sum_b), ("half", "grp", "tile"))
    mean_a = total_a.astype(BF)
    mean_b = total_b.astype(BF)
    kinetic_part = kinetic_columns(kinetic, orbitals)
    rows_x, rows_y, width_all = orbitals.shape
    width_a = mean_a.shape[1]
    width_b = mean_b.shape[1]
    stack_a = jnp.transpose(mean_a, (1, 0, 2)).reshape(width_a, TERMS * width_a)
    stack_b = jnp.transpose(mean_b, (1, 0, 2)).reshape(width_b, TERMS * width_b)
    points = orbitals.reshape(rows_x * rows_y, width_all)
    weights = potential.reshape(2, TERMS, rows_x * rows_y)
    action = point_action(points, weights, stack_a, stack_b).reshape(rows_x, rows_y, width_all)
    return (kinetic_part.astype(F32) + action).astype(BF)


VMEM = pl.BlockSpec(memory_space=pltpu.VMEM)
SMEM = pl.BlockSpec(memory_space=pltpu.SMEM)


def place_matrix(me, flips, side, turned):
    groups = side.groups
    per, step = side.rows // groups, side.points
    count = len(flips) * per * step
    shape = (step * side.rows, count) if turned else (count, step * side.rows)
    to = lax.broadcasted_iota(jnp.int32, shape, 1 if turned else 0)
    source = lax.broadcasted_iota(jnp.int32, shape, 0 if turned else 1)
    flip = jnp.zeros(shape, jnp.int32)
    for at, value in enumerate(flips):
        flip = jnp.where(to // (per * step) == at, value, flip)
    wanted = (to % step) * side.rows + (me ^ flip) * per + (to // step) % per
    return jnp.where(wanted == source, 1.0, 0.0).astype(BF)


def slot_kernel(terms_ref, oper_ref, core_ref, out_ref, core_f, core_t, core_p, mixed):
    rows, width_b, width_a = core_ref.shape
    width = out_ref.shape[2]
    slots = terms_ref.shape[1]
    out_ref[...] = jnp.zeros_like(out_ref)
    mixed[...] = jnp.zeros_like(mixed)
    core_p[...] = jnp.zeros_like(core_p)
    core_p[:, :, :width_a] = core_ref[...]
    core_f[...] = core_p[...].astype(F32)
    core_t[...] = jnp.transpose(core_f[...].reshape(rows * width_b, width)).astype(BF)
    live = jnp.int32(0)
    for slot in range(slots):
        live = live + (terms_ref[0, slot] < TERMS).astype(jnp.int32)

    def one_slot(slot, carry):
        def one_block(block, inner):
            start = pl.multiple_of(block * 16, 16)
            source = [core_f[r, pl.ds(start, 16), :] for r in range(rows)]
            for q in range(rows):
                total = source[0] * oper_ref[slot, q]
                for r in range(1, rows):
                    total = total + source[r] * oper_ref[slot, r * rows + q]
                mixed[q, pl.ds(width_a + start, 16), :] = total.astype(BF)
            return inner

        lax.fori_loop(0, width_b // 16, one_block, 0)
        flat = mixed[:, width_a:, :].reshape(rows * width_b, width)
        gram_a = jnp.dot(core_t[:width_a, :], flat, preferred_element_type=F32)
        gram_b = jnp.zeros((width_b, width), F32)
        for q in range(rows):
            gram_b = gram_b + lax.dot_general(
                core_p[q], mixed[q], (((1,), (1,)), ((), ())), preferred_element_type=F32
            )
        term = terms_ref[0, slot]
        out_ref[term, :width_b, :] = (gram_a[:width_b] + gram_b).astype(BF)
        out_ref[term, width_b:, :] = gram_a[width_b:].astype(BF)
        return carry

    lax.fori_loop(0, live, one_slot, 0)


def tile_mean_fields(core_tensor, term_operators, block_terms):
    rows, width_b, width_a = core_tensor.shape
    slots = block_terms.shape[1]
    width = width_a + width_b
    operators = term_operators.astype(F32).reshape(slots, rows * rows)
    return pl.pallas_call(
        slot_kernel,
        out_shape=jax.ShapeDtypeStruct((TERMS, width_a, width), BF),
        in_specs=[SMEM, SMEM, VMEM],
        out_specs=VMEM,
        scratch_shapes=[
            pltpu.VMEM((rows, width_b, width), F32),
            pltpu.VMEM((width, rows * width_b), BF),
            pltpu.VMEM((rows, width_b, width), BF),
            pltpu.VMEM((rows, width, width), BF),
        ],
        cost_estimate=pl.CostEstimate(flops=10**9, bytes_accessed=2 * 10**6, transcendentals=0),
        name="slot_sums",
    )(block_terms, operators, core_tensor)


def exchange(array, axes, flip):
    count = lax.axis_size(axes)
    return lax.ppermute(array, axes, [(i, i ^ flip) for i in range(count)])


def scatter_sum(array, axes, place, flips):
    rows = array.shape[0] // (len(flips) + 1)

    def block(index):
        return lax.dynamic_slice_in_dim(array, index * rows, rows, 0)

    arrived = [exchange(block(place ^ own), axes, flip) for flip, own in flips]
    total = block(place).astype(F32)
    for part in arrived:
        total = total + part.astype(F32)
    return total.astype(BF)


def gather_blocks(array, axes, place, flips):
    rows = array.shape[0]
    whole = jnp.zeros((rows * (len(flips) + 1),) + array.shape[1:], array.dtype)
    arrived = [(own, exchange(array, axes, flip)) for flip, own in flips]
    whole = lax.dynamic_update_slice_in_dim(whole, array, place * rows, 0)
    for own, part in arrived:
        whole = lax.dynamic_update_slice_in_dim(whole, part, (place ^ own) * rows, 0)
    return whole


def bit_flips(bits):
    flips = []
    for own in range(1, 1 << len(bits)):
        flip = sum(1 << bit for at, bit in enumerate(bits) if own >> at & 1)
        flips.append((flip, own))
    return flips


def place_of(index, bits):
    place = jnp.int32(0)
    for at, bit in enumerate(bits):
        place = place | (((index >> bit) & 1) << at)
    return place


def total_mean_fields(partial, potential):
    terms, width_a, width = partial.shape
    group_index = lax.axis_index(GROUP)
    tile_index = lax.axis_index("tile")
    tile_bits = list(range(lax.axis_size("tile").bit_length() - 1))
    group_bits = list(range(lax.axis_size(GROUP).bit_length() - 1))
    far = lax.axis_size("grp").bit_length() - 2
    near = [bit for bit in group_bits if bit != far]
    stages = [("tile", tile_index, tile_bits), (GROUP, group_index, near)]
    array = partial.reshape(terms * width_a, width)
    for axes, index, bits in stages:
        array = scatter_sum(array, axes, place_of(index, bits), bit_flips(bits))
    array = (array.astype(F32) + exchange(array, GROUP, 1 << far).astype(F32)).astype(BF)
    for axes, index, bits in reversed(stages):
        array = gather_blocks(array, axes, place_of(index, bits), bit_flips(bits))
        array, potential = lax.optimization_barrier((array, potential))
    return array.reshape(terms, width_a, width), potential


def action_kernel(on_chip, points_ref, weight_ref, mean_ref, out_ref, blocks):
    width_a = mean_ref.shape[1]
    count_x, rows, width = points_ref.shape
    width_b = width - width_a

    @pl.when(pl.program_id(0) == 0)
    def _():
        lane = lax.broadcasted_iota(jnp.int32, (width_a, width), 1)
        for term in range(TERMS):
            packed = mean_ref[term].astype(F32)
            blocks[term, :width_a, :] = jnp.where(lane < width_a, packed, 0.0).astype(BF)
            blocks[term, width_a:, :] = jnp.where(
                lane[:width_b] < width_a, 0.0, packed[:width_b]
            ).astype(BF)

    step = 16
    while count_x % step or step * rows > 512:
        step //= 2
    base = pl.program_id(0) * count_x if on_chip else 0
    count = step * rows
    on_a = lax.broadcasted_iota(jnp.int32, (count, width), 1) < width_a
    for start in range(0, count_x, step):
        points = points_ref[start : start + step].reshape(count, width)
        weight = weight_ref[start : start + step].reshape(count, 2 * TERMS)
        scaled = []
        for term in range(TERMS):
            weight_a = weight[:, term : term + 1]
            weight_b = weight[:, TERMS + term : TERMS + term + 1]
            scaled.append(points * jnp.where(on_a, weight_a, weight_b))
        total = jnp.dot(
            jnp.concatenate(scaled, axis=1),
            blocks[...].reshape(TERMS * width, width),
            preferred_element_type=F32,
        )
        out_ref[pl.ds(base + start, step)] = total.reshape(step, rows, width)


def action_rows(orbitals, weights, mean, first_row, rows, on_chip):
    rows_x, _, width = orbitals.shape
    step = min(rows_x, 1024 // rows // 8 * 8)
    while rows_x % step:
        step -= 8
    at = first_row // rows
    out = (rows_x, rows, width)
    block = pl.BlockSpec((step, rows, width), lambda i: (i, 0, 0))
    return pl.pallas_call(
        functools.partial(action_kernel, on_chip),
        grid=(rows_x // step,),
        out_shape=pltpu.VMEM(out, F32) if on_chip else jax.ShapeDtypeStruct(out, F32),
        in_specs=[
            pl.BlockSpec((step, rows, width), lambda i: (i, at, 0)),
            pl.BlockSpec((step, rows, 2 * TERMS), lambda i: (i, at, 0)),
            pl.BlockSpec(mean.shape, lambda i: (0, 0, 0)),
        ],
        out_specs=VMEM if on_chip else block,
        scratch_shapes=[pltpu.VMEM((TERMS, width, width), BF)],
        cost_estimate=pl.CostEstimate(
            flops=2 * rows_x * rows * width * width * TERMS,
            bytes_accessed=8 * rows_x * rows * width,
            transcendentals=0,
        ),
        name="action",
    )(orbitals, weights, mean)


class Side(NamedTuple):
    groups: int
    rows: int
    points: int


def side_of(groups):
    rows = max(8, groups)
    return Side(groups, rows, LANES // rows)


def block_rows(first_row, chunk, side):
    rows = side.rows
    while chunk % (2 * rows) == 0 and first_row % (2 * rows) == 0 and rows < 32:
        rows *= 2
    return rows


def split_kernel(flips, side, me_ref, orb_ref, *refs):
    outs, matrix = refs[:-1], refs[-1]
    rows_x, rows, width = orb_ref.shape
    per, step = side.rows // side.groups, side.points

    @pl.when(pl.program_id(0) == 0)
    def _():
        matrix[...] = place_matrix(me_ref[0], flips, side, False)

    for part in range(rows // side.rows):
        for start in range(0, rows_x, step):
            block = orb_ref[start : start + step, part * side.rows : (part + 1) * side.rows, :]
            moved = jnp.dot(
                matrix[...], block.reshape(step * side.rows, width), preferred_element_type=F32
            )
            moved = moved.astype(BF).reshape(len(flips), per, step, width)
            for at in range(len(flips)):
                outs[at][part * per : (part + 1) * per, start : start + step, :] = moved[at]


def split_chunk(me, orbitals, first_row, chunk, flips, side):
    rows_x, _, width = orbitals.shape
    rows = block_rows(first_row, chunk, side)
    piece = (rows // side.groups, rows_x, width)
    on_chip = rows == chunk and len(flips) < side.groups
    kind = pltpu.VMEM if on_chip else jax.ShapeDtypeStruct
    return pl.pallas_call(
        functools.partial(split_kernel, tuple(flips), side),
        grid=(chunk // rows,),
        out_shape=[kind((chunk // side.groups, rows_x, width), BF)] * len(flips),
        in_specs=[
            SMEM,
            pl.BlockSpec((rows_x, rows, width), lambda p: (0, first_row // rows + p, 0)),
        ],
        out_specs=[VMEM if on_chip else pl.BlockSpec(piece, lambda p: (p, 0, 0))] * len(flips),
        scratch_shapes=[pltpu.VMEM((len(flips) * LANES // side.groups, LANES), BF)],
        cost_estimate=pl.CostEstimate(
            flops=2 * rows_x * chunk * width * LANES,
            bytes_accessed=4 * rows_x * chunk * width,
            transcendentals=0,
        ),
        name="split",
    )(me, orbitals)


def apply_kernel(groups, me_ref, kin_ref, *refs):
    pieces, outs = refs[:groups], refs[groups : 2 * groups]
    gathered, result = refs[2 * groups :]
    _, rows_x, _ = pieces[0].shape
    size_x = kin_ref.shape[0]
    me = me_ref[0]
    for flip in range(groups):
        start = pl.multiple_of((me ^ flip) * rows_x, rows_x)
        gathered[pl.ds(start, rows_x), :] = pieces[flip][0]
    step = 512
    for start in range(0, size_x, step):
        applied = jnp.dot(
            kin_ref[start : start + step, :], gathered[...], preferred_element_type=F32
        )
        result[start : start + step, :] = applied.astype(BF)
    for flip in range(groups):
        start = pl.multiple_of((me ^ flip) * rows_x, rows_x)
        outs[flip][0] = result[pl.ds(start, rows_x), :]


def apply_chunk(me, kinetic, pieces):
    groups = len(pieces)
    per, rows_x, width = pieces[0].shape
    size_x = kinetic.shape[0]
    block = pl.BlockSpec((1, rows_x, width), lambda i: (i, 0, 0))
    whole = pl.BlockSpec((size_x, size_x), lambda i: (0, 0), pipeline_mode=pl.Buffered(1))
    return pl.pallas_call(
        functools.partial(apply_kernel, groups),
        grid=(per,),
        out_shape=[jax.ShapeDtypeStruct((per, rows_x, width), BF)] * groups,
        in_specs=[SMEM, whole] + [block] * groups,
        out_specs=[block] * groups,
        scratch_shapes=[pltpu.VMEM((size_x, width), BF)] * 2,
        cost_estimate=pl.CostEstimate(
            flops=2 * size_x * size_x * per * width, bytes_accessed=4 * 10**6, transcendentals=0
        ),
        name="apply",
    )(me, kinetic, *pieces)


def join_kernel(side, me_ref, action_ref, *refs):
    pieces = refs[: side.groups]
    out_ref, matrix = refs[-2:]
    step_x, rows, width = out_ref.shape
    per, step = side.rows // side.groups, side.points

    @pl.when((pl.program_id(0) == 0) & (pl.program_id(1) == 0))
    def _():
        matrix[...] = place_matrix(me_ref[0], range(side.groups), side, True)

    for part in range(rows // side.rows):
        here = slice(part * side.rows, (part + 1) * side.rows)
        for start in range(0, step_x, step):
            block = jnp.concatenate(
                [
                    piece[part * per : (part + 1) * per, start : start + step, :]
                    for piece in pieces
                ],
                axis=0,
            ).reshape(step * side.rows, width)
            moved = jnp.dot(matrix[...], block, preferred_element_type=F32)
            total = moved.reshape(step, side.rows, width) + action_ref[start : start + step, here, :]
            out_ref[start : start + step, here, :] = total.astype(BF)


def join_chunk(me, action, pieces, first_row, before, rows_y, side):
    groups = len(pieces)
    _, rows_x, width = pieces[0].shape
    chunk = pieces[0].shape[0] * groups
    rows = block_rows(first_row, chunk, side)
    step_x = rows_x // 2 if chunk == rows else rows_x
    block = pl.BlockSpec((step_x, rows, width), lambda p, i: (i, first_row // rows + p, 0))
    piece = pl.BlockSpec((rows // groups, step_x, width), lambda p, i: (p, i, 0))
    in_specs = [SMEM, block] + [piece] * groups
    operands = [me, action, *pieces]
    aliases = {}
    if before is not None:
        in_specs.append(pl.BlockSpec(memory_space=pl.ANY))
        aliases = {len(operands): 0}
        operands.append(before)
    return pl.pallas_call(
        functools.partial(join_kernel, side),
        grid=(chunk // rows, rows_x // step_x),
        out_shape=jax.ShapeDtypeStruct((rows_x, rows_y, width), BF),
        in_specs=in_specs,
        out_specs=block,
        scratch_shapes=[pltpu.VMEM((LANES, LANES), BF)],
        input_output_aliases=aliases,
        cost_estimate=pl.CostEstimate(
            flops=2 * rows_x * chunk * width * LANES,
            bytes_accessed=8 * rows_x * chunk * width,
            transcendentals=0,
        ),
        name="join",
    )(*operands)


def last_join_kernel(side, first_row, me_ref, action_ref, *refs):
    pieces = refs[: side.groups]
    out_ref, matrix, parts, sems = refs[-4:]
    rows_x, rows, width = action_ref.shape
    per, step = side.rows // side.groups, side.points
    matrix[...] = place_matrix(me_ref[0], range(side.groups), side, True)
    copies = []
    for at, start in enumerate(range(0, rows_x, step)):
        for part in range(rows // side.rows):
            here = slice(part * side.rows, (part + 1) * side.rows)
            block = jnp.concatenate(
                [
                    piece[part * per : (part + 1) * per, start : start + step, :]
                    for piece in pieces
                ],
                axis=0,
            ).reshape(step * side.rows, width)
            moved = jnp.dot(matrix[...], block, preferred_element_type=F32)
            total = moved.reshape(step, side.rows, width) + action_ref[start : start + step, here, :]
            parts[at, :, here, :] = total.astype(BF)
        where = out_ref.at[pl.ds(start, step), pl.ds(first_row, rows), :]
        copies.append(pltpu.make_async_copy(parts.at[at], where, sems.at[at]))
        copies[-1].start()
    for copy in copies:
        copy.wait()


def last_join(me, action, pieces, first_row, before, side):
    rows_x, rows, width = action.shape
    blocks = rows_x // side.points
    pieces = [pltpu.with_memory_space_constraint(piece, pltpu.VMEM) for piece in pieces]
    action = pltpu.with_memory_space_constraint(action, pltpu.VMEM)
    hbm = pl.BlockSpec(memory_space=pl.ANY)
    return pl.pallas_call(
        functools.partial(last_join_kernel, side, first_row),
        out_shape=jax.ShapeDtypeStruct(before.shape, BF),
        in_specs=[SMEM] + [VMEM] * (1 + len(pieces)) + [hbm],
        out_specs=hbm,
        scratch_shapes=[
            pltpu.VMEM((LANES, LANES), BF),
            pltpu.VMEM((blocks, side.points, rows, width), BF),
            pltpu.SemaphoreType.DMA((blocks,)),
        ],
        input_output_aliases={2 + len(pieces): 0},
        cost_estimate=pl.CostEstimate(
            flops=2 * rows_x * rows * width * LANES,
            bytes_accessed=2 * rows_x * rows * width,
            transcendentals=0,
        ),
        name="join",
    )(me, action, *pieces, before)


def far_flip():
    return lax.axis_size("grp") // 2


def exchange_some(pieces, flips):
    return {flip: exchange(pieces[flip], GROUP, flip) if flip else pieces[0] for flip in flips}


def exchange_all(pieces, near_first):
    far = far_flip()
    order = sorted(range(len(pieces)), key=lambda flip: (bool(flip & far) == near_first, flip))
    arrived = exchange_some(pieces, order)
    return [arrived[flip] for flip in range(len(pieces))]


def chunk_sizes(rows_y, side):
    if rows_y % (4 * side.rows):
        return [side.rows] * (rows_y // side.rows)
    return [rows_y // 2, rows_y // 4, rows_y // 4]


def chunked_body(core_tensor, term_operators, block_terms, orbitals, potential, kinetic):
    rows_x, rows_y, _ = orbitals.shape
    groups = lax.axis_size(GROUP)
    side = side_of(groups)
    sizes = chunk_sizes(rows_y, side)
    first_rows = [sum(sizes[:index]) for index in range(len(sizes))]
    far = [flip for flip in range(groups) if flip & far_flip()]
    near = [flip for flip in range(groups) if flip not in far]
    me = lax.axis_index(GROUP).astype(jnp.int32).reshape(1)
    returned = []
    for index, (first, size) in enumerate(zip(first_rows, sizes)):
        if index == 0:
            arrived = {}
            for flips in (far, near):
                cut = split_chunk(me, orbitals, first, size, flips, side)
                arrived.update(exchange_some(dict(zip(flips, cut)), flips))
            pieces = [arrived[flip] for flip in range(groups)]
        else:
            pieces = split_chunk(me, orbitals, first, size, range(groups), side)
            pieces = exchange_all(pieces, True)
        pieces = apply_chunk(me, kinetic, pieces)
        returned.append(exchange_all(pieces, True))
    partial = tile_mean_fields(core_tensor, term_operators, block_terms)
    mean, potential = total_mean_fields(partial, potential)
    last_row, last_rows = first_rows[-1], sizes[-1]
    weights = potential.reshape(2 * TERMS, rows_x * rows_y).T.astype(BF)
    weights = weights.reshape(rows_x, rows_y, 2 * TERMS)
    action = action_rows(orbitals, weights, mean, 0, last_row, False)
    action_last = action_rows(orbitals, weights, mean, last_row, last_rows, True)
    result = None
    for index, first in enumerate(first_rows[:-1]):
        result = join_chunk(me, action, returned[index], first, result, rows_y, side)
    result = last_join(me, action_last, returned[-1], last_row, result, side)
    return result


def fits(core_tensor, orbitals, mesh):
    rows_x, rows_y, width = orbitals
    groups = mesh.shape["half"] * mesh.shape["grp"]
    tiles = mesh.shape["tile"]
    _, width_b, width_a = core_tensor
    return (
        mesh.shape["half"] == 2
        and mesh.shape["grp"] >= 2
        and groups & (groups - 1) == 0
        and tiles & (tiles - 1) == 0
        and tiles > 1
        and groups % 8 == 0
        and LANES % (2 * groups) == 0
        and rows_y % groups == 0
        and rows_x % 128 == 0
        and width == width_a + width_b
        and width % 256 == 0
        and width_b % 16 == 0
        and width_a % 16 == 0
        and width_b <= width_a
        and TERMS * width_a % (groups * tiles * 8) == 0
    )


def solution(mesh):
    specs = (
        P(("half", "grp", "tile"), None, None),
        P(("half", "grp", "tile"), None, None, None),
        P(("half", "grp", "tile"), None),
        P(("half", "grp"), "tile", None),
        P(None, None, ("half", "grp"), "tile"),
        P(),
    )

    def build(body):
        return jax.shard_map(body, mesh=mesh, in_specs=specs, out_specs=specs[3], check_vma=False)

    def whole(core_tensor, term_operators, block_terms, orbitals, potential, kinetic):
        args = (core_tensor, term_operators, block_terms, orbitals, potential, kinetic)
        size_x, size_y, width = orbitals.shape
        rows_x = size_x // (mesh.shape["half"] * mesh.shape["grp"])
        rows_y = size_y // mesh.shape["tile"]
        if not fits(core_tensor.shape, (rows_x, rows_y, width), mesh):
            return build(plain_body)(*args)
        return build(chunked_body)(*args)

    return whole
```

```python
import functools
from typing import NamedTuple

import jax
import jax.numpy as jnp
from jax import lax
from jax.experimental import pallas as pl
from jax.experimental.pallas import tpu as pltpu
from jax.sharding import PartitionSpec as P


TERMS = 8
GROUP = ("half", "grp")
LANES = 256
HALF = 128
BF = jnp.bfloat16
F32 = jnp.float32


def slot_sums(core_tensor, term_operators, block_terms):
    rows_tile, width_b, width_a = core_tensor.shape
    flat_core = core_tensor.reshape(rows_tile, width_b * width_a)
    listed = block_terms[0]
    live_slots = jnp.sum((listed < TERMS).astype(jnp.int32))
    labels = jnp.arange(TERMS, dtype=jnp.int32)

    def add_slot(slot_index, running):
        sum_a, sum_b = running
        operator = term_operators[0, slot_index]
        mixed_core = jnp.einsum("rs,rq->sq", operator, flat_core, preferred_element_type=F32)
        mixed_core = mixed_core.astype(BF).reshape(rows_tile, width_b, width_a)
        gram_a = jnp.einsum("rba,rbc->ac", core_tensor, mixed_core, preferred_element_type=F32)
        gram_b = jnp.einsum("rba,rda->bd", core_tensor, mixed_core, preferred_element_type=F32)
        chosen = (labels == listed[slot_index]).astype(F32)
        return (sum_a + chosen[:, None, None] * gram_a, sum_b + chosen[:, None, None] * gram_b)

    start_sums = (
        jnp.zeros((TERMS, width_a, width_a), F32),
        jnp.zeros((TERMS, width_b, width_b), F32),
    )
    return lax.fori_loop(0, live_slots, add_slot, start_sums)


def point_action(points, weights, stack_a, stack_b):
    width_a = stack_a.shape[0]
    width_b = stack_b.shape[0]
    count_points = points.shape[0]
    prod_a = jnp.dot(points[:, :width_a], stack_a, preferred_element_type=F32).reshape(
        count_points, TERMS, width_a
    )
    prod_b = jnp.dot(points[:, width_a:], stack_b, preferred_element_type=F32).reshape(
        count_points, TERMS, width_b
    )
    act_a = jnp.sum(prod_a * weights[0].T[:, :, None], axis=1)
    act_b = jnp.sum(prod_b * weights[1].T[:, :, None], axis=1)
    return jnp.concatenate([act_a, act_b], axis=1)


def kinetic_columns(kinetic, orbitals):
    rows_x, rows_y, width_all = orbitals.shape
    groups = lax.axis_size("half") * lax.axis_size("grp")
    columns = rows_y * width_all // groups
    pieces = orbitals.reshape(rows_x, groups, columns)
    applied = jnp.einsum(
        "xz,zik->xik",
        kinetic,
        lax.all_to_all(pieces, GROUP, split_axis=1, concat_axis=0, tiled=True),
        preferred_element_type=F32,
    )
    applied = applied.astype(BF)
    returned = lax.all_to_all(applied, GROUP, split_axis=0, concat_axis=1, tiled=True)
    return returned.reshape(rows_x, rows_y, width_all)


def plain_body(core_tensor, term_operators, block_terms, orbitals, potential, kinetic):
    sum_a, sum_b = slot_sums(core_tensor, term_operators, block_terms)
    total_a, total_b = lax.psum((sum_a, sum_b), ("half", "grp", "tile"))
    mean_a = total_a.astype(BF)
    mean_b = total_b.astype(BF)
    kinetic_part = kinetic_columns(kinetic, orbitals)
    rows_x, rows_y, width_all = orbitals.shape
    width_a = mean_a.shape[1]
    width_b = mean_b.shape[1]
    stack_a = jnp.transpose(mean_a, (1, 0, 2)).reshape(width_a, TERMS * width_a)
    stack_b = jnp.transpose(mean_b, (1, 0, 2)).reshape(width_b, TERMS * width_b)
    points = orbitals.reshape(rows_x * rows_y, width_all)
    weights = potential.reshape(2, TERMS, rows_x * rows_y)
    action = point_action(points, weights, stack_a, stack_b).reshape(rows_x, rows_y, width_all)
    return (kinetic_part.astype(F32) + action).astype(BF)


VMEM = pl.BlockSpec(memory_space=pltpu.VMEM)
SMEM = pl.BlockSpec(memory_space=pltpu.SMEM)


def place_matrix(me, flips, side, turned):
    groups = side.groups
    per, step = side.rows // groups, side.points
    count = len(flips) * per * step
    shape = (step * side.rows, count) if turned else (count, step * side.rows)
    to = lax.broadcasted_iota(jnp.int32, shape, 1 if turned else 0)
    source = lax.broadcasted_iota(jnp.int32, shape, 0 if turned else 1)
    flip = jnp.zeros(shape, jnp.int32)
    for at, value in enumerate(flips):
        flip = jnp.where(to // (per * step) == at, value, flip)
    wanted = (to % step) * side.rows + (me ^ flip) * per + (to // step) % per
    return jnp.where(wanted == source, 1.0, 0.0).astype(BF)


def packed_rows(width_a, width_b):
    each = width_a + width_b
    beside = HALF // (width_a - HALF)
    return each, TERMS * each + TERMS // beside * (width_a - width_b)


def slot_kernel(terms_ref, oper_ref, core_ref, out_ref, core_f, core_t, core_p, mixed, rest):
    rows, width_b, width_a = core_ref.shape
    width = width_a + width_b
    each, _ = packed_rows(width_a, width_b)
    extra = width_a - HALF
    beside = HALF // extra
    rest[...] = jnp.zeros_like(rest)
    slots = terms_ref.shape[1]
    out_ref[...] = jnp.zeros_like(out_ref)
    mixed[...] = jnp.zeros_like(mixed)
    core_p[...] = jnp.zeros_like(core_p)
    core_p[:, :, :width_a] = core_ref[...]
    core_f[...] = core_p[...].astype(F32)
    core_t[...] = jnp.transpose(core_f[...].reshape(rows * width_b, width)).astype(BF)
    live = jnp.int32(0)
    for slot in range(slots):
        live = live + (terms_ref[0, slot] < TERMS).astype(jnp.int32)

    def one_slot(slot, carry):
        def one_block(block, inner):
            start = pl.multiple_of(block * 16, 16)
            source = [core_f[r, pl.ds(start, 16), :] for r in range(rows)]
            for q in range(rows):
                total = source[0] * oper_ref[slot, q]
                for r in range(1, rows):
                    total = total + source[r] * oper_ref[slot, r * rows + q]
                mixed[q, pl.ds(width_a + start, 16), :] = total.astype(BF)
            return inner

        lax.fori_loop(0, width_b // 16, one_block, 0)
        flat = mixed[:, width_a:, :].reshape(rows * width_b, width)
        gram_a = jnp.dot(core_t[:width_a, :], flat, preferred_element_type=F32)
        gram_b = jnp.zeros((width_b, width), F32)
        for q in range(rows):
            gram_b = gram_b + lax.dot_general(
                core_p[q], mixed[q], (((1,), (1,)), ((), ())), preferred_element_type=F32
            )
        term = terms_ref[0, slot]
        at = pl.multiple_of(term * each, 16)
        out_ref[pl.ds(at, width_a), :] = gram_a[:, :HALF].astype(BF)
        both = gram_a[:width_b, HALF:] + gram_b[:, HALF:]
        out_ref[pl.ds(at + width_a, width_b), :] = both.astype(BF)
        moved = pltpu.roll(gram_a[width_b:, HALF:], (term % beside) * extra, 1)
        rest[term // beside] = rest[term // beside] + moved
        return carry

    lax.fori_loop(0, live, one_slot, 0)
    count, tail, _ = rest.shape
    out_ref[TERMS * each :, :] = rest[...].reshape(count * tail, HALF).astype(BF)


def tile_mean_fields(core_tensor, term_operators, block_terms):
    rows, width_b, width_a = core_tensor.shape
    slots = block_terms.shape[1]
    width = width_a + width_b
    operators = term_operators.astype(F32).reshape(slots, rows * rows)
    return pl.pallas_call(
        slot_kernel,
        out_shape=jax.ShapeDtypeStruct((packed_rows(width_a, width_b)[1], HALF), BF),
        in_specs=[SMEM, SMEM, VMEM],
        out_specs=VMEM,
        scratch_shapes=[
            pltpu.VMEM((rows, width_b, width), F32),
            pltpu.VMEM((width, rows * width_b), BF),
            pltpu.VMEM((rows, width_b, width), BF),
            pltpu.VMEM((rows, width, width), BF),
            pltpu.VMEM((TERMS * (width_a - HALF) // HALF, width_a - width_b, HALF), F32),
        ],
        cost_estimate=pl.CostEstimate(flops=10**9, bytes_accessed=2 * 10**6, transcendentals=0),
        name="slot_sums",
    )(block_terms, operators, core_tensor)


def exchange(array, axes, flip):
    count = lax.axis_size(axes)
    return lax.ppermute(array, axes, [(i, i ^ flip) for i in range(count)])


def scatter_sum(array, axes, place, flips):
    rows = array.shape[0] // (len(flips) + 1)

    def block(index):
        return lax.dynamic_slice_in_dim(array, index * rows, rows, 0)

    arrived = [exchange(block(place ^ own), axes, flip) for flip, own in flips]
    total = block(place).astype(F32)
    for part in arrived:
        total = total + part.astype(F32)
    return total.astype(BF)


def gather_blocks(array, axes, place, flips):
    rows = array.shape[0]
    whole = jnp.zeros((rows * (len(flips) + 1),) + array.shape[1:], array.dtype)
    arrived = [(own, exchange(array, axes, flip)) for flip, own in flips]
    whole = lax.dynamic_update_slice_in_dim(whole, array, place * rows, 0)
    for own, part in arrived:
        whole = lax.dynamic_update_slice_in_dim(whole, part, (place ^ own) * rows, 0)
    return whole


def bit_flips(bits):
    flips = []
    for own in range(1, 1 << len(bits)):
        flip = sum(1 << bit for at, bit in enumerate(bits) if own >> at & 1)
        flips.append((flip, own))
    return flips


def place_of(index, bits):
    place = jnp.int32(0)
    for at, bit in enumerate(bits):
        place = place | (((index >> bit) & 1) << at)
    return place


def total_mean_fields(partial, potential):
    group_index = lax.axis_index(GROUP)
    tile_index = lax.axis_index("tile")
    tile_bits = list(range(lax.axis_size("tile").bit_length() - 1))
    group_bits = list(range(lax.axis_size(GROUP).bit_length() - 1))
    far = lax.axis_size("grp").bit_length() - 2
    near = [bit for bit in group_bits if bit != far]
    stages = [("tile", tile_index, tile_bits), (GROUP, group_index, near)]
    array = partial
    for axes, index, bits in stages:
        array = scatter_sum(array, axes, place_of(index, bits), bit_flips(bits))
    array = (array.astype(F32) + exchange(array, GROUP, 1 << far).astype(F32)).astype(BF)
    for axes, index, bits in reversed(stages):
        array = gather_blocks(array, axes, place_of(index, bits), bit_flips(bits))
        array, potential = lax.optimization_barrier((array, potential))
    return array, potential


def action_kernel(width_a, on_chip, points_ref, weight_ref, mean_ref, out_ref, blocks):
    count_x, rows, width = points_ref.shape
    width_b = width - width_a
    each, _ = packed_rows(width_a, width_b)
    extra = width_a - HALF
    beside, tail = HALF // extra, width_a - width_b

    @pl.when(pl.program_id(0) == 0)
    def _():
        blocks[...] = jnp.zeros_like(blocks)
        for term in range(TERMS):
            at = term * each
            blocks[term, :width_a, :HALF] = mean_ref[at : at + width_a, :]
            both = mean_ref[at + width_a : at + each, :].astype(F32)
            lane = lax.broadcasted_iota(jnp.int32, (width_b, HALF), 1)
            blocks[term, :width_b, HALF:] = jnp.where(lane < extra, both, 0.0).astype(BF)
            blocks[term, width_a:, HALF:] = jnp.where(lane < extra, 0.0, both).astype(BF)
            start = TERMS * each + term // beside * tail
            other = mean_ref[start : start + tail, :].astype(F32)
            other = pltpu.roll(other, (HALF - term % beside * extra) % HALF, 1)
            blocks[term, width_b:width_a, HALF:] = jnp.where(lane[:tail] < extra, other, 0.0).astype(BF)

    step = 16
    while count_x % step or step * rows > 512:
        step //= 2
    base = pl.program_id(0) * count_x if on_chip else 0
    count = step * rows
    on_a = lax.broadcasted_iota(jnp.int32, (count, width), 1) < width_a
    for start in range(0, count_x, step):
        points = points_ref[start : start + step].reshape(count, width)
        weight = weight_ref[start : start + step].reshape(count, 2 * TERMS)
        scaled = []
        for term in range(TERMS):
            weight_a = weight[:, term : term + 1]
            weight_b = weight[:, TERMS + term : TERMS + term + 1]
            scaled.append(points * jnp.where(on_a, weight_a, weight_b))
        total = jnp.dot(
            jnp.concatenate(scaled, axis=1),
            blocks[...].reshape(TERMS * width, width),
            preferred_element_type=F32,
        )
        out_ref[pl.ds(base + start, step)] = total.reshape(step, rows, width)


def action_rows(width_a, orbitals, weights, mean, first_row, rows, on_chip):
    rows_x, _, width = orbitals.shape
    step = min(rows_x, 1024 // rows // 8 * 8)
    while rows_x % step:
        step -= 8
    at = first_row // rows
    out = (rows_x, rows, width)
    block = pl.BlockSpec((step, rows, width), lambda i: (i, 0, 0))
    return pl.pallas_call(
        functools.partial(action_kernel, width_a, on_chip),
        grid=(rows_x // step,),
        out_shape=pltpu.VMEM(out, F32) if on_chip else jax.ShapeDtypeStruct(out, F32),
        in_specs=[
            pl.BlockSpec((step, rows, width), lambda i: (i, at, 0)),
            pl.BlockSpec((step, rows, 2 * TERMS), lambda i: (i, at, 0)),
            pl.BlockSpec(mean.shape, lambda i: (0, 0)),
        ],
        out_specs=VMEM if on_chip else block,
        scratch_shapes=[pltpu.VMEM((TERMS, width, width), BF)],
        cost_estimate=pl.CostEstimate(
            flops=2 * rows_x * rows * width * width * TERMS,
            bytes_accessed=8 * rows_x * rows * width,
            transcendentals=0,
        ),
        name="action",
    )(orbitals, weights, mean)


class Side(NamedTuple):
    groups: int
    rows: int
    points: int


def side_of(groups):
    rows = max(8, groups)
    return Side(groups, rows, LANES // rows)


def block_rows(first_row, chunk, side):
    rows = side.rows
    while chunk % (2 * rows) == 0 and first_row % (2 * rows) == 0 and rows < 32:
        rows *= 2
    return rows


def split_kernel(flips, side, me_ref, orb_ref, *refs):
    outs, matrix = refs[:-1], refs[-1]
    rows_x, rows, width = orb_ref.shape
    per, step = side.rows // side.groups, side.points

    @pl.when(pl.program_id(0) == 0)
    def _():
        matrix[...] = place_matrix(me_ref[0], flips, side, False)

    for part in range(rows // side.rows):
        for start in range(0, rows_x, step):
            block = orb_ref[start : start + step, part * side.rows : (part + 1) * side.rows, :]
            moved = jnp.dot(
                matrix[...], block.reshape(step * side.rows, width), preferred_element_type=F32
            )
            moved = moved.astype(BF).reshape(len(flips), per, step, width)
            for at in range(len(flips)):
                outs[at][part * per : (part + 1) * per, start : start + step, :] = moved[at]


def split_chunk(me, orbitals, first_row, chunk, flips, side):
    rows_x, _, width = orbitals.shape
    rows = block_rows(first_row, chunk, side)
    piece = (rows // side.groups, rows_x, width)
    on_chip = rows == chunk and len(flips) < side.groups
    kind = pltpu.VMEM if on_chip else jax.ShapeDtypeStruct
    return pl.pallas_call(
        functools.partial(split_kernel, tuple(flips), side),
        grid=(chunk // rows,),
        out_shape=[kind((chunk // side.groups, rows_x, width), BF)] * len(flips),
        in_specs=[
            SMEM,
            pl.BlockSpec((rows_x, rows, width), lambda p: (0, first_row // rows + p, 0)),
        ],
        out_specs=[VMEM if on_chip else pl.BlockSpec(piece, lambda p: (p, 0, 0))] * len(flips),
        scratch_shapes=[pltpu.VMEM((len(flips) * LANES // side.groups, LANES), BF)],
        cost_estimate=pl.CostEstimate(
            flops=2 * rows_x * chunk * width * LANES,
            bytes_accessed=4 * rows_x * chunk * width,
            transcendentals=0,
        ),
        name="split",
    )(me, orbitals)


def apply_kernel(groups, me_ref, kin_ref, *refs):
    pieces, outs = refs[:groups], refs[groups : 2 * groups]
    gathered, result = refs[2 * groups :]
    _, rows_x, _ = pieces[0].shape
    size_x = kin_ref.shape[0]
    me = me_ref[0]
    for flip in range(groups):
        start = pl.multiple_of((me ^ flip) * rows_x, rows_x)
        gathered[pl.ds(start, rows_x), :] = pieces[flip][0]
    step = 512
    for start in range(0, size_x, step):
        applied = jnp.dot(
            kin_ref[start : start + step, :], gathered[...], preferred_element_type=F32
        )
        result[start : start + step, :] = applied.astype(BF)
    for flip in range(groups):
        start = pl.multiple_of((me ^ flip) * rows_x, rows_x)
        outs[flip][0] = result[pl.ds(start, rows_x), :]


def apply_chunk(me, kinetic, pieces):
    groups = len(pieces)
    per, rows_x, width = pieces[0].shape
    size_x = kinetic.shape[0]
    block = pl.BlockSpec((1, rows_x, width), lambda i: (i, 0, 0))
    whole = pl.BlockSpec((size_x, size_x), lambda i: (0, 0), pipeline_mode=pl.Buffered(1))
    return pl.pallas_call(
        functools.partial(apply_kernel, groups),
        grid=(per,),
        out_shape=[jax.ShapeDtypeStruct((per, rows_x, width), BF)] * groups,
        in_specs=[SMEM, whole] + [block] * groups,
        out_specs=[block] * groups,
        scratch_shapes=[pltpu.VMEM((size_x, width), BF)] * 2,
        cost_estimate=pl.CostEstimate(
            flops=2 * size_x * size_x * per * width, bytes_accessed=4 * 10**6, transcendentals=0
        ),
        name="apply",
    )(me, kinetic, *pieces)


def join_kernel(side, me_ref, action_ref, *refs):
    pieces = refs[: side.groups]
    out_ref, matrix = refs[-2:]
    step_x, rows, width = out_ref.shape
    per, step = side.rows // side.groups, side.points

    @pl.when((pl.program_id(0) == 0) & (pl.program_id(1) == 0))
    def _():
        matrix[...] = place_matrix(me_ref[0], range(side.groups), side, True)

    for part in range(rows // side.rows):
        here = slice(part * side.rows, (part + 1) * side.rows)
        for start in range(0, step_x, step):
            block = jnp.concatenate(
                [
                    piece[part * per : (part + 1) * per, start : start + step, :]
                    for piece in pieces
                ],
                axis=0,
            ).reshape(step * side.rows, width)
            moved = jnp.dot(matrix[...], block, preferred_element_type=F32)
            total = moved.reshape(step, side.rows, width) + action_ref[start : start + step, here, :]
            out_ref[start : start + step, here, :] = total.astype(BF)


def join_chunk(me, action, pieces, first_row, before, rows_y, side):
    groups = len(pieces)
    _, rows_x, width = pieces[0].shape
    chunk = pieces[0].shape[0] * groups
    rows = block_rows(first_row, chunk, side)
    step_x = rows_x // 2 if chunk == rows else rows_x
    block = pl.BlockSpec((step_x, rows, width), lambda p, i: (i, first_row // rows + p, 0))
    piece = pl.BlockSpec((rows // groups, step_x, width), lambda p, i: (p, i, 0))
    in_specs = [SMEM, block] + [piece] * groups
    operands = [me, action, *pieces]
    aliases = {}
    if before is not None:
        in_specs.append(pl.BlockSpec(memory_space=pl.ANY))
        aliases = {len(operands): 0}
        operands.append(before)
    return pl.pallas_call(
        functools.partial(join_kernel, side),
        grid=(chunk // rows, rows_x // step_x),
        out_shape=jax.ShapeDtypeStruct((rows_x, rows_y, width), BF),
        in_specs=in_specs,
        out_specs=block,
        scratch_shapes=[pltpu.VMEM((LANES, LANES), BF)],
        input_output_aliases=aliases,
        cost_estimate=pl.CostEstimate(
            flops=2 * rows_x * chunk * width * LANES,
            bytes_accessed=8 * rows_x * chunk * width,
            transcendentals=0,
        ),
        name="join",
    )(*operands)


def last_join_kernel(side, first_row, me_ref, action_ref, *refs):
    pieces = refs[: side.groups]
    out_ref, matrix, parts, sems = refs[-4:]
    rows_x, rows, width = action_ref.shape
    per, step = side.rows // side.groups, side.points
    matrix[...] = place_matrix(me_ref[0], range(side.groups), side, True)
    copies = []
    for at, start in enumerate(range(0, rows_x, step)):
        for part in range(rows // side.rows):
            here = slice(part * side.rows, (part + 1) * side.rows)
            block = jnp.concatenate(
                [
                    piece[part * per : (part + 1) * per, start : start + step, :]
                    for piece in pieces
                ],
                axis=0,
            ).reshape(step * side.rows, width)
            moved = jnp.dot(matrix[...], block, preferred_element_type=F32)
            total = moved.reshape(step, side.rows, width) + action_ref[start : start + step, here, :]
            parts[at, :, here, :] = total.astype(BF)
        where = out_ref.at[pl.ds(start, step), pl.ds(first_row, rows), :]
        copies.append(pltpu.make_async_copy(parts.at[at], where, sems.at[at]))
        copies[-1].start()
    for copy in copies:
        copy.wait()


def last_join(me, action, pieces, first_row, before, side):
    rows_x, rows, width = action.shape
    blocks = rows_x // side.points
    pieces = [pltpu.with_memory_space_constraint(piece, pltpu.VMEM) for piece in pieces]
    action = pltpu.with_memory_space_constraint(action, pltpu.VMEM)
    hbm = pl.BlockSpec(memory_space=pl.ANY)
    return pl.pallas_call(
        functools.partial(last_join_kernel, side, first_row),
        out_shape=jax.ShapeDtypeStruct(before.shape, BF),
        in_specs=[SMEM] + [VMEM] * (1 + len(pieces)) + [hbm],
        out_specs=hbm,
        scratch_shapes=[
            pltpu.VMEM((LANES, LANES), BF),
            pltpu.VMEM((blocks, side.points, rows, width), BF),
            pltpu.SemaphoreType.DMA((blocks,)),
        ],
        input_output_aliases={2 + len(pieces): 0},
        cost_estimate=pl.CostEstimate(
            flops=2 * rows_x * rows * width * LANES,
            bytes_accessed=2 * rows_x * rows * width,
            transcendentals=0,
        ),
        name="join",
    )(me, action, *pieces, before)


def far_flip():
    return lax.axis_size("grp") // 2


def exchange_some(pieces, flips):
    return {flip: exchange(pieces[flip], GROUP, flip) if flip else pieces[0] for flip in flips}


def exchange_all(pieces, near_first):
    far = far_flip()
    order = sorted(range(len(pieces)), key=lambda flip: (bool(flip & far) == near_first, flip))
    arrived = exchange_some(pieces, order)
    return [arrived[flip] for flip in range(len(pieces))]


def chunk_sizes(rows_y, side):
    if rows_y % (4 * side.rows):
        return [side.rows] * (rows_y // side.rows)
    return [rows_y // 2, rows_y // 4, rows_y // 4]


def chunked_body(core_tensor, term_operators, block_terms, orbitals, potential, kinetic):
    rows_x, rows_y, _ = orbitals.shape
    groups = lax.axis_size(GROUP)
    side = side_of(groups)
    sizes = chunk_sizes(rows_y, side)
    first_rows = [sum(sizes[:index]) for index in range(len(sizes))]
    far = [flip for flip in range(groups) if flip & far_flip()]
    near = [flip for flip in range(groups) if flip not in far]
    me = lax.axis_index(GROUP).astype(jnp.int32).reshape(1)
    returned = []
    for index, (first, size) in enumerate(zip(first_rows, sizes)):
        if index == 0:
            arrived = {}
            for flips in (far, near):
                cut = split_chunk(me, orbitals, first, size, flips, side)
                arrived.update(exchange_some(dict(zip(flips, cut)), flips))
            pieces = [arrived[flip] for flip in range(groups)]
        else:
            pieces = split_chunk(me, orbitals, first, size, range(groups), side)
            pieces = exchange_all(pieces, True)
        pieces = apply_chunk(me, kinetic, pieces)
        returned.append(exchange_all(pieces, True))
    partial = tile_mean_fields(core_tensor, term_operators, block_terms)
    mean, potential = total_mean_fields(partial, potential)
    last_row, last_rows = first_rows[-1], sizes[-1]
    weights = potential.reshape(2 * TERMS, rows_x * rows_y).T.astype(BF)
    weights = weights.reshape(rows_x, rows_y, 2 * TERMS)
    width_a = core_tensor.shape[2]
    action = action_rows(width_a, orbitals, weights, mean, 0, last_row, False)
    action_last = action_rows(
        width_a, orbitals, weights, mean, last_row, last_rows, True
    )
    result = None
    for index, first in enumerate(first_rows[:-1]):
        result = join_chunk(me, action, returned[index], first, result, rows_y, side)
    result = last_join(me, action_last, returned[-1], last_row, result, side)
    return result


def fits(core_tensor, orbitals, mesh):
    rows_x, rows_y, width = orbitals
    groups = mesh.shape["half"] * mesh.shape["grp"]
    tiles = mesh.shape["tile"]
    _, width_b, width_a = core_tensor
    return (
        mesh.shape["half"] == 2
        and mesh.shape["grp"] >= 2
        and groups & (groups - 1) == 0
        and tiles & (tiles - 1) == 0
        and tiles > 1
        and groups % 8 == 0
        and LANES % (2 * groups) == 0
        and rows_y % groups == 0
        and rows_x % 128 == 0
        and width == width_a + width_b
        and width % 256 == 0
        and width_b % 16 == 0
        and width_a % 16 == 0
        and width_b <= width_a
        and width == 2 * HALF
        and width_a > HALF
        and HALF % (width_a - HALF) == 0
        and TERMS % (HALF // (width_a - HALF)) == 0
        and width_a - width_b <= width_b
        and packed_rows(width_a, width_b)[1] % (groups // 2 * tiles * 8) == 0
    )


def solution(mesh):
    specs = (
        P(("half", "grp", "tile"), None, None),
        P(("half", "grp", "tile"), None, None, None),
        P(("half", "grp", "tile"), None),
        P(("half", "grp"), "tile", None),
        P(None, None, ("half", "grp"), "tile"),
        P(),
    )

    def build(body):
        return jax.shard_map(body, mesh=mesh, in_specs=specs, out_specs=specs[3], check_vma=False)

    def whole(core_tensor, term_operators, block_terms, orbitals, potential, kinetic):
        args = (core_tensor, term_operators, block_terms, orbitals, potential, kinetic)
        size_x, size_y, width = orbitals.shape
        rows_x = size_x // (mesh.shape["half"] * mesh.shape["grp"])
        rows_y = size_y // mesh.shape["tile"]
        if not fits(core_tensor.shape, (rows_x, rows_y, width), mesh):
            return build(plain_body)(*args)
        return build(chunked_body)(*args)

    return whole
```

```python
import functools
from typing import NamedTuple

import jax
import jax.numpy as jnp
from jax import lax
from jax.experimental import pallas as pl
from jax.experimental.pallas import tpu as pltpu
from jax.sharding import PartitionSpec as P


TERMS = 8
GROUP = ("half", "grp")
LANES = 256
BF = jnp.bfloat16
F32 = jnp.float32


def slot_sums(core_tensor, term_operators, block_terms):
    rows_tile, width_b, width_a = core_tensor.shape
    flat_core = core_tensor.reshape(rows_tile, width_b * width_a)
    listed = block_terms[0]
    live_slots = jnp.sum((listed < TERMS).astype(jnp.int32))
    labels = jnp.arange(TERMS, dtype=jnp.int32)

    def add_slot(slot_index, running):
        sum_a, sum_b = running
        operator = term_operators[0, slot_index]
        mixed_core = jnp.einsum("rs,rq->sq", operator, flat_core, preferred_element_type=F32)
        mixed_core = mixed_core.astype(BF).reshape(rows_tile, width_b, width_a)
        gram_a = jnp.einsum("rba,rbc->ac", core_tensor, mixed_core, preferred_element_type=F32)
        gram_b = jnp.einsum("rba,rda->bd", core_tensor, mixed_core, preferred_element_type=F32)
        chosen = (labels == listed[slot_index]).astype(F32)
        return (sum_a + chosen[:, None, None] * gram_a, sum_b + chosen[:, None, None] * gram_b)

    start_sums = (
        jnp.zeros((TERMS, width_a, width_a), F32),
        jnp.zeros((TERMS, width_b, width_b), F32),
    )
    return lax.fori_loop(0, live_slots, add_slot, start_sums)


def point_action(points, weights, stack_a, stack_b):
    width_a = stack_a.shape[0]
    width_b = stack_b.shape[0]
    count_points = points.shape[0]
    prod_a = jnp.dot(points[:, :width_a], stack_a, preferred_element_type=F32).reshape(
        count_points, TERMS, width_a
    )
    prod_b = jnp.dot(points[:, width_a:], stack_b, preferred_element_type=F32).reshape(
        count_points, TERMS, width_b
    )
    act_a = jnp.sum(prod_a * weights[0].T[:, :, None], axis=1)
    act_b = jnp.sum(prod_b * weights[1].T[:, :, None], axis=1)
    return jnp.concatenate([act_a, act_b], axis=1)


def kinetic_columns(kinetic, orbitals):
    rows_x, rows_y, width_all = orbitals.shape
    groups = lax.axis_size("half") * lax.axis_size("grp")
    columns = rows_y * width_all // groups
    pieces = orbitals.reshape(rows_x, groups, columns)
    applied = jnp.einsum(
        "xz,zik->xik",
        kinetic,
        lax.all_to_all(pieces, GROUP, split_axis=1, concat_axis=0, tiled=True),
        preferred_element_type=F32,
    )
    applied = applied.astype(BF)
    returned = lax.all_to_all(applied, GROUP, split_axis=0, concat_axis=1, tiled=True)
    return returned.reshape(rows_x, rows_y, width_all)


def plain_body(core_tensor, term_operators, block_terms, orbitals, potential, kinetic):
    sum_a, sum_b = slot_sums(core_tensor, term_operators, block_terms)
    total_a, total_b = lax.psum((sum_a, sum_b), ("half", "grp", "tile"))
    mean_a = total_a.astype(BF)
    mean_b = total_b.astype(BF)
    kinetic_part = kinetic_columns(kinetic, orbitals)
    rows_x, rows_y, width_all = orbitals.shape
    width_a = mean_a.shape[1]
    width_b = mean_b.shape[1]
    stack_a = jnp.transpose(mean_a, (1, 0, 2)).reshape(width_a, TERMS * width_a)
    stack_b = jnp.transpose(mean_b, (1, 0, 2)).reshape(width_b, TERMS * width_b)
    points = orbitals.reshape(rows_x * rows_y, width_all)
    weights = potential.reshape(2, TERMS, rows_x * rows_y)
    action = point_action(points, weights, stack_a, stack_b).reshape(rows_x, rows_y, width_all)
    return (kinetic_part.astype(F32) + action).astype(BF)


VMEM = pl.BlockSpec(memory_space=pltpu.VMEM)
SMEM = pl.BlockSpec(memory_space=pltpu.SMEM)


def place_matrix(me, flips, side, turned):
    groups = side.groups
    per, step = side.rows // groups, side.points
    count = len(flips) * per * step
    shape = (step * side.rows, count) if turned else (count, step * side.rows)
    to = lax.broadcasted_iota(jnp.int32, shape, 1 if turned else 0)
    source = lax.broadcasted_iota(jnp.int32, shape, 0 if turned else 1)
    flip = jnp.zeros(shape, jnp.int32)
    for at, value in enumerate(flips):
        flip = jnp.where(to // (per * step) == at, value, flip)
    wanted = (to % step) * side.rows + (me ^ flip) * per + (to // step) % per
    return jnp.where(wanted == source, 1.0, 0.0).astype(BF)


def slot_kernel(terms_ref, oper_ref, core_ref, out_ref, core_f, core_t, core_p, mixed):
    rows, width_b, width_a = core_ref.shape
    width = out_ref.shape[2]
    slots = terms_ref.shape[1]
    out_ref[...] = jnp.zeros_like(out_ref)
    mixed[...] = jnp.zeros_like(mixed)
    core_p[...] = jnp.zeros_like(core_p)
    core_p[:, :, :width_a] = core_ref[...]
    core_f[...] = core_p[...].astype(F32)
    core_t[...] = jnp.transpose(core_f[...].reshape(rows * width_b, width)).astype(BF)
    live = jnp.int32(0)
    for slot in range(slots):
        live = live + (terms_ref[0, slot] < TERMS).astype(jnp.int32)

    def one_slot(slot, carry):
        def one_block(block, inner):
            start = pl.multiple_of(block * 16, 16)
            source = [core_f[r, pl.ds(start, 16), :] for r in range(rows)]
            for q in range(rows):
                total = source[0] * oper_ref[slot, q]
                for r in range(1, rows):
                    total = total + source[r] * oper_ref[slot, r * rows + q]
                mixed[q, pl.ds(width_a + start, 16), :] = total.astype(BF)
            return inner

        lax.fori_loop(0, width_b // 16, one_block, 0)
        flat = mixed[:, width_a:, :].reshape(rows * width_b, width)
        gram_a = jnp.dot(core_t[:width_a, :], flat, preferred_element_type=F32)
        gram_b = jnp.zeros((width_b, width), F32)
        for q in range(rows):
            gram_b = gram_b + lax.dot_general(
                core_p[q], mixed[q], (((1,), (1,)), ((), ())), preferred_element_type=F32
            )
        term = terms_ref[0, slot]
        out_ref[term, :width_b, :] = (gram_a[:width_b] + gram_b).astype(BF)
        out_ref[term, width_b:, :] = gram_a[width_b:].astype(BF)
        return carry

    lax.fori_loop(0, live, one_slot, 0)


def tile_mean_fields(core_tensor, term_operators, block_terms):
    rows, width_b, width_a = core_tensor.shape
    slots = block_terms.shape[1]
    width = width_a + width_b
    operators = term_operators.astype(F32).reshape(slots, rows * rows)
    return pl.pallas_call(
        slot_kernel,
        out_shape=jax.ShapeDtypeStruct((TERMS, width_a, width), BF),
        in_specs=[SMEM, SMEM, VMEM],
        out_specs=VMEM,
        scratch_shapes=[
            pltpu.VMEM((rows, width_b, width), F32),
            pltpu.VMEM((width, rows * width_b), BF),
            pltpu.VMEM((rows, width_b, width), BF),
            pltpu.VMEM((rows, width, width), BF),
        ],
        cost_estimate=pl.CostEstimate(flops=10**9, bytes_accessed=2 * 10**6, transcendentals=0),
        name="slot_sums",
    )(block_terms, operators, core_tensor)


def exchange(array, axes, flip):
    count = lax.axis_size(axes)
    return lax.ppermute(array, axes, [(i, i ^ flip) for i in range(count)])


def scatter_sum(array, axes, place, flips):
    rows = array.shape[0] // (len(flips) + 1)

    def block(index):
        return lax.dynamic_slice_in_dim(array, index * rows, rows, 0)

    arrived = [exchange(block(place ^ own), axes, flip) for flip, own in flips]
    total = block(place).astype(F32)
    for part in arrived:
        total = total + part.astype(F32)
    return total.astype(BF)


def gather_blocks(array, axes, place, flips):
    rows = array.shape[0]
    whole = jnp.zeros((rows * (len(flips) + 1),) + array.shape[1:], array.dtype)
    arrived = [(own, exchange(array, axes, flip)) for flip, own in flips]
    whole = lax.dynamic_update_slice_in_dim(whole, array, place * rows, 0)
    for own, part in arrived:
        whole = lax.dynamic_update_slice_in_dim(whole, part, (place ^ own) * rows, 0)
    return whole


def bit_flips(bits):
    flips = []
    for own in range(1, 1 << len(bits)):
        flip = sum(1 << bit for at, bit in enumerate(bits) if own >> at & 1)
        flips.append((flip, own))
    return flips


def place_of(index, bits):
    place = jnp.int32(0)
    for at, bit in enumerate(bits):
        place = place | (((index >> bit) & 1) << at)
    return place


def total_mean_fields(partial, potential):
    terms, width_a, width = partial.shape
    group_index = lax.axis_index(GROUP)
    tile_index = lax.axis_index("tile")
    tile_bits = list(range(lax.axis_size("tile").bit_length() - 1))
    group_bits = list(range(lax.axis_size(GROUP).bit_length() - 1))
    far = lax.axis_size("grp").bit_length() - 2
    near = [bit for bit in group_bits if bit != far]
    stages = [("tile", tile_index, tile_bits), (GROUP, group_index, near)]
    array = partial.reshape(terms * width_a, width)
    for axes, index, bits in stages:
        array = scatter_sum(array, axes, place_of(index, bits), bit_flips(bits))
    array = (array.astype(F32) + exchange(array, GROUP, 1 << far).astype(F32)).astype(BF)
    for axes, index, bits in reversed(stages):
        array = gather_blocks(array, axes, place_of(index, bits), bit_flips(bits))
        array, potential = lax.optimization_barrier((array, potential))
    return array.reshape(terms, width_a, width), potential


def action_kernel(on_chip, points_ref, weight_ref, mean_ref, out_ref, blocks):
    width_a = mean_ref.shape[1]
    count_x, rows, width = points_ref.shape
    width_b = width - width_a

    @pl.when(pl.program_id(0) == 0)
    def _():
        lane = lax.broadcasted_iota(jnp.int32, (width_a, width), 1)
        for term in range(TERMS):
            packed = mean_ref[term].astype(F32)
            blocks[term, :width_a, :] = jnp.where(lane < width_a, packed, 0.0).astype(BF)
            blocks[term, width_a:, :] = jnp.where(
                lane[:width_b] < width_a, 0.0, packed[:width_b]
            ).astype(BF)

    step = 16
    while count_x % step or step * rows > 512:
        step //= 2
    base = pl.program_id(0) * count_x if on_chip else 0
    count = step * rows
    on_a = lax.broadcasted_iota(jnp.int32, (count, width), 1) < width_a
    for start in range(0, count_x, step):
        points = points_ref[start : start + step].reshape(count, width)
        weight = weight_ref[start : start + step].reshape(count, 2 * TERMS)
        scaled = []
        for term in range(TERMS):
            weight_a = weight[:, term : term + 1]
            weight_b = weight[:, TERMS + term : TERMS + term + 1]
            scaled.append(points * jnp.where(on_a, weight_a, weight_b))
        total = jnp.dot(
            jnp.concatenate(scaled, axis=1),
            blocks[...].reshape(TERMS * width, width),
            preferred_element_type=F32,
        )
        out_ref[pl.ds(base + start, step)] = total.reshape(step, rows, width)


def action_rows(orbitals, weights, mean, first_row, rows, on_chip):
    rows_x, _, width = orbitals.shape
    step = min(rows_x, 1024 // rows // 8 * 8)
    while rows_x % step:
        step -= 8
    at = first_row // rows
    out = (rows_x, rows, width)
    block = pl.BlockSpec((step, rows, width), lambda i: (i, 0, 0))
    return pl.pallas_call(
        functools.partial(action_kernel, on_chip),
        grid=(rows_x // step,),
        out_shape=pltpu.VMEM(out, F32) if on_chip else jax.ShapeDtypeStruct(out, F32),
        in_specs=[
            pl.BlockSpec((step, rows, width), lambda i: (i, at, 0)),
            pl.BlockSpec((step, rows, 2 * TERMS), lambda i: (i, at, 0)),
            pl.BlockSpec(mean.shape, lambda i: (0, 0, 0)),
        ],
        out_specs=VMEM if on_chip else block,
        scratch_shapes=[pltpu.VMEM((TERMS, width, width), BF)],
        cost_estimate=pl.CostEstimate(
            flops=2 * rows_x * rows * width * width * TERMS,
            bytes_accessed=8 * rows_x * rows * width,
            transcendentals=0,
        ),
        name="action",
    )(orbitals, weights, mean)


class Side(NamedTuple):
    groups: int
    rows: int
    points: int


def side_of(groups):
    rows = max(8, groups)
    return Side(groups, rows, LANES // rows)


def block_rows(first_row, chunk, side):
    rows = side.rows
    while chunk % (2 * rows) == 0 and first_row % (2 * rows) == 0 and rows < 32:
        rows *= 2
    return rows


def split_kernel(flips, side, me_ref, orb_ref, *refs):
    outs, matrix = refs[:-1], refs[-1]
    rows_x, rows, width = orb_ref.shape
    per, step = side.rows // side.groups, side.points

    @pl.when(pl.program_id(0) == 0)
    def _():
        matrix[...] = place_matrix(me_ref[0], flips, side, False)

    for part in range(rows // side.rows):
        for start in range(0, rows_x, step):
            block = orb_ref[start : start + step, part * side.rows : (part + 1) * side.rows, :]
            moved = jnp.dot(
                matrix[...], block.reshape(step * side.rows, width), preferred_element_type=F32
            )
            moved = moved.astype(BF).reshape(len(flips), per, step, width)
            for at in range(len(flips)):
                outs[at][part * per : (part + 1) * per, start : start + step, :] = moved[at]


def split_chunk(me, orbitals, first_row, chunk, flips, side):
    rows_x, _, width = orbitals.shape
    rows = block_rows(first_row, chunk, side)
    piece = (rows // side.groups, rows_x, width)
    on_chip = rows == chunk and len(flips) < side.groups
    kind = pltpu.VMEM if on_chip else jax.ShapeDtypeStruct
    return pl.pallas_call(
        functools.partial(split_kernel, tuple(flips), side),
        grid=(chunk // rows,),
        out_shape=[kind((chunk // side.groups, rows_x, width), BF)] * len(flips),
        in_specs=[
            SMEM,
            pl.BlockSpec((rows_x, rows, width), lambda p: (0, first_row // rows + p, 0)),
        ],
        out_specs=[VMEM if on_chip else pl.BlockSpec(piece, lambda p: (p, 0, 0))] * len(flips),
        scratch_shapes=[pltpu.VMEM((len(flips) * LANES // side.groups, LANES), BF)],
        cost_estimate=pl.CostEstimate(
            flops=2 * rows_x * chunk * width * LANES,
            bytes_accessed=4 * rows_x * chunk * width,
            transcendentals=0,
        ),
        name="split",
    )(me, orbitals)


def apply_kernel(order, me_ref, kin_ref, *refs):
    groups = len(order)
    pieces, outs = refs[:groups], refs[groups : 2 * groups]
    gathered, result = refs[2 * groups :]
    _, rows_x, _ = pieces[0].shape
    size_x = kin_ref.shape[0]
    me = me_ref[0]
    for slot, flip in enumerate(order):
        start = pl.multiple_of((me ^ flip) * rows_x, rows_x)
        gathered[pl.ds(start, rows_x), :] = pieces[slot][0]
    step = 512
    for start in range(0, size_x, step):
        applied = jnp.dot(
            kin_ref[start : start + step, :], gathered[...], preferred_element_type=F32
        )
        result[start : start + step, :] = applied.astype(BF)
    for slot, flip in enumerate(order):
        start = pl.multiple_of((me ^ flip) * rows_x, rows_x)
        outs[slot][0] = result[pl.ds(start, rows_x), :]


def apply_chunk(me, kinetic, pieces, order):
    groups = len(pieces)
    per, rows_x, width = pieces[0].shape
    size_x = kinetic.shape[0]
    block = pl.BlockSpec((1, rows_x, width), lambda i: (i, 0, 0))
    whole = pl.BlockSpec((size_x, size_x), lambda i: (0, 0), pipeline_mode=pl.Buffered(1))
    return pl.pallas_call(
        functools.partial(apply_kernel, order),
        grid=(per,),
        out_shape=[jax.ShapeDtypeStruct((per, rows_x, width), BF)] * groups,
        in_specs=[SMEM, whole] + [block] * groups,
        out_specs=[block] * groups,
        scratch_shapes=[pltpu.VMEM((size_x, width), BF)] * 2,
        cost_estimate=pl.CostEstimate(
            flops=2 * size_x * size_x * per * width, bytes_accessed=4 * 10**6, transcendentals=0
        ),
        name="apply",
    )(me, kinetic, *pieces)


def join_kernel(side, order, me_ref, action_ref, *refs):
    pieces = refs[: side.groups]
    out_ref, matrix = refs[-2:]
    step_x, rows, width = out_ref.shape
    per, step = side.rows // side.groups, side.points

    @pl.when((pl.program_id(0) == 0) & (pl.program_id(1) == 0))
    def _():
        matrix[...] = place_matrix(me_ref[0], order, side, True)

    for part in range(rows // side.rows):
        here = slice(part * side.rows, (part + 1) * side.rows)
        for start in range(0, step_x, step):
            block = jnp.concatenate(
                [
                    piece[part * per : (part + 1) * per, start : start + step, :]
                    for piece in pieces
                ],
                axis=0,
            ).reshape(step * side.rows, width)
            moved = jnp.dot(matrix[...], block, preferred_element_type=F32)
            total = moved.reshape(step, side.rows, width) + action_ref[start : start + step, here, :]
            out_ref[start : start + step, here, :] = total.astype(BF)


def join_chunk(me, action, pieces, first_row, before, rows_y, side, order):
    groups = len(pieces)
    _, rows_x, width = pieces[0].shape
    chunk = pieces[0].shape[0] * groups
    rows = block_rows(first_row, chunk, side)
    step_x = rows_x // 2 if chunk == rows else rows_x
    block = pl.BlockSpec((step_x, rows, width), lambda p, i: (i, first_row // rows + p, 0))
    piece = pl.BlockSpec((rows // groups, step_x, width), lambda p, i: (p, i, 0))
    in_specs = [SMEM, block] + [piece] * groups
    operands = [me, action, *pieces]
    aliases = {}
    if before is not None:
        in_specs.append(pl.BlockSpec(memory_space=pl.ANY))
        aliases = {len(operands): 0}
        operands.append(before)
    return pl.pallas_call(
        functools.partial(join_kernel, side, order),
        grid=(chunk // rows, rows_x // step_x),
        out_shape=jax.ShapeDtypeStruct((rows_x, rows_y, width), BF),
        in_specs=in_specs,
        out_specs=block,
        scratch_shapes=[pltpu.VMEM((LANES, LANES), BF)],
        input_output_aliases=aliases,
        cost_estimate=pl.CostEstimate(
            flops=2 * rows_x * chunk * width * LANES,
            bytes_accessed=8 * rows_x * chunk * width,
            transcendentals=0,
        ),
        name="join",
    )(*operands)


def last_join_kernel(side, order, first_row, me_ref, action_ref, *refs):
    pieces = refs[: side.groups]
    out_ref, matrix, parts, sems = refs[-4:]
    rows_x, rows, width = action_ref.shape
    per, step = side.rows // side.groups, side.points
    matrix[...] = place_matrix(me_ref[0], order, side, True)
    copies = []
    for at, start in enumerate(range(0, rows_x, step)):
        for part in range(rows // side.rows):
            here = slice(part * side.rows, (part + 1) * side.rows)
            block = jnp.concatenate(
                [
                    piece[part * per : (part + 1) * per, start : start + step, :]
                    for piece in pieces
                ],
                axis=0,
            ).reshape(step * side.rows, width)
            moved = jnp.dot(matrix[...], block, preferred_element_type=F32)
            total = moved.reshape(step, side.rows, width) + action_ref[start : start + step, here, :]
            parts[at, :, here, :] = total.astype(BF)
        where = out_ref.at[pl.ds(start, step), pl.ds(first_row, rows), :]
        copies.append(pltpu.make_async_copy(parts.at[at], where, sems.at[at]))
        copies[-1].start()
    for copy in copies:
        copy.wait()


def last_join(me, action, pieces, first_row, before, side, order):
    rows_x, rows, width = action.shape
    blocks = rows_x // side.points
    pieces = [pltpu.with_memory_space_constraint(piece, pltpu.VMEM) for piece in pieces]
    action = pltpu.with_memory_space_constraint(action, pltpu.VMEM)
    hbm = pl.BlockSpec(memory_space=pl.ANY)
    return pl.pallas_call(
        functools.partial(last_join_kernel, side, order, first_row),
        out_shape=jax.ShapeDtypeStruct(before.shape, BF),
        in_specs=[SMEM] + [VMEM] * (1 + len(pieces)) + [hbm],
        out_specs=hbm,
        scratch_shapes=[
            pltpu.VMEM((LANES, LANES), BF),
            pltpu.VMEM((blocks, side.points, rows, width), BF),
            pltpu.SemaphoreType.DMA((blocks,)),
        ],
        input_output_aliases={2 + len(pieces): 0},
        cost_estimate=pl.CostEstimate(
            flops=2 * rows_x * rows * width * LANES,
            bytes_accessed=2 * rows_x * rows * width,
            transcendentals=0,
        ),
        name="join",
    )(me, action, *pieces, before)


def far_flip():
    return lax.axis_size("grp") // 2


def exchange_some(pieces, flips):
    return {flip: exchange(pieces[flip], GROUP, flip) if flip else pieces[0] for flip in flips}


def exchange_all(pieces, order):
    return [exchange(piece, GROUP, flip) if flip else piece for piece, flip in zip(pieces, order)]


def chunk_sizes(rows_y, side):
    if rows_y % (4 * side.rows):
        return [side.rows] * (rows_y // side.rows)
    return [rows_y // 2, rows_y // 4, rows_y // 4]


def chunked_body(core_tensor, term_operators, block_terms, orbitals, potential, kinetic):
    rows_x, rows_y, _ = orbitals.shape
    groups = lax.axis_size(GROUP)
    side = side_of(groups)
    sizes = chunk_sizes(rows_y, side)
    first_rows = [sum(sizes[:index]) for index in range(len(sizes))]
    far = [flip for flip in range(groups) if flip & far_flip()]
    near = [flip for flip in range(groups) if flip not in far]
    order = tuple(far + near)
    me = lax.axis_index(GROUP).astype(jnp.int32).reshape(1)
    returned = []
    for index, (first, size) in enumerate(zip(first_rows, sizes)):
        if index == 0:
            arrived = {}
            for flips in (far, near):
                cut = split_chunk(me, orbitals, first, size, flips, side)
                arrived.update(exchange_some(dict(zip(flips, cut)), flips))
            pieces = [arrived[flip] for flip in order]
        else:
            pieces = split_chunk(me, orbitals, first, size, order, side)
            pieces = exchange_all(pieces, order)
        pieces = apply_chunk(me, kinetic, pieces, order)
        returned.append(exchange_all(pieces, order))
    partial = tile_mean_fields(core_tensor, term_operators, block_terms)
    mean, potential = total_mean_fields(partial, potential)
    last_row, last_rows = first_rows[-1], sizes[-1]
    weights = potential.reshape(2 * TERMS, rows_x * rows_y).T.astype(BF)
    weights = weights.reshape(rows_x, rows_y, 2 * TERMS)
    action = action_rows(orbitals, weights, mean, 0, last_row, False)
    action_last = action_rows(orbitals, weights, mean, last_row, last_rows, True)
    result = None
    for index, first in enumerate(first_rows[:-1]):
        result = join_chunk(
            me, action, returned[index], first, result, rows_y, side, order
        )
    result = last_join(me, action_last, returned[-1], last_row, result, side, order)
    return result


def fits(core_tensor, orbitals, mesh):
    rows_x, rows_y, width = orbitals
    groups = mesh.shape["half"] * mesh.shape["grp"]
    tiles = mesh.shape["tile"]
    _, width_b, width_a = core_tensor
    return (
        mesh.shape["half"] == 2
        and mesh.shape["grp"] >= 2
        and groups & (groups - 1) == 0
        and tiles & (tiles - 1) == 0
        and tiles > 1
        and groups % 8 == 0
        and LANES % (2 * groups) == 0
        and rows_y % groups == 0
        and rows_x % 128 == 0
        and width == width_a + width_b
        and width % 256 == 0
        and width_b % 16 == 0
        and width_a % 16 == 0
        and width_b <= width_a
        and TERMS * width_a % (groups * tiles * 8) == 0
    )


def solution(mesh):
    specs = (
        P(("half", "grp", "tile"), None, None),
        P(("half", "grp", "tile"), None, None, None),
        P(("half", "grp", "tile"), None),
        P(("half", "grp"), "tile", None),
        P(None, None, ("half", "grp"), "tile"),
        P(),
    )

    def build(body):
        return jax.shard_map(body, mesh=mesh, in_specs=specs, out_specs=specs[3], check_vma=False)

    def whole(core_tensor, term_operators, block_terms, orbitals, potential, kinetic):
        args = (core_tensor, term_operators, block_terms, orbitals, potential, kinetic)
        size_x, size_y, width = orbitals.shape
        rows_x = size_x // (mesh.shape["half"] * mesh.shape["grp"])
        rows_y = size_y // mesh.shape["tile"]
        if not fits(core_tensor.shape, (rows_x, rows_y, width), mesh):
            return build(plain_body)(*args)
        return build(chunked_body)(*args)

    return whole
```
